256 devices in a mesh: seq: 128 (over x, z, y), head: 2 (over core).
Axes of the slice: x: 4, y: 4, z: 8, core: 2. Of those that a mesh axis runs over, the one named last changes fastest.
Arguments:
- queries: bfloat16 [16384, 1024], P('seq', 'head'), may hold values from -6 to 6
- key_rows: bfloat16 [16384, 1024], P('seq', 'head'), may hold values from -6 to 6
- values: bfloat16 [16384, 2048], P('seq', 'head'), may hold values from -6 to 6
- out_gate: bfloat16 [16384, 2048], P('seq', 'head'), may hold values from -6 to 6
- write_rate: float32 [16, 16384], P('head', 'seq'), may hold values from 0 to 1
- log_decay: float32 [16, 16384], P('head', 'seq'), may hold values from -1 to 0, as said below
- norm_gain: float32 [128], replicated, may hold values from 0.1 to 1.9
- out_weight: bfloat16 [2048, 2048], P('head'), may hold values from -0.125 to 0.125
Outputs:
- layer_out: bfloat16 [16384, 2048], P('seq', 'head')
The draws below stay inside these ranges and needn't reach their ends.
Inputs may be any that keep to these rules, and one draw needn't show every extreme that they name: `log_decay`: log decay of each value head and token, negative.
All inputs are finite; a program needn't handle non-finite values.
Results may differ from the reference program's by a relative error of at most 0.009.
Values may be sent and summed in bfloat16 or wider, within the bound.
A program may use at most 320 MiB of HBM per device.

```python
import math
import jax
import jax.numpy as jnp
from jax import lax

D = 2048
VALUE_HEAD_COUNT = 16
HK = 8
DK = 128
DV = 128
SPAN = 64
TOK_DEV = 128
PROMPT_TOKENS = 16384


def slow_heads(key):
    share = 0.5
    return jax.random.uniform(jax.random.fold_in(key, 11), (VALUE_HEAD_COUNT,)) < share


def draw_write_rate(key, part):
    sluggish_mask = slow_heads(key)
    fast_vals = jax.random.uniform(jax.random.fold_in(key, 23), (VALUE_HEAD_COUNT, PROMPT_TOKENS), jnp.float32, 0.3, 0.9)
    slow_log = jax.random.uniform(jax.random.fold_in(key, 29), (VALUE_HEAD_COUNT, PROMPT_TOKENS), jnp.float32, math.log(0.25), math.log(0.6))
    slow_vals = jnp.exp(slow_log) * (DK / PROMPT_TOKENS)
    return jnp.where(sluggish_mask[:, None], slow_vals, fast_vals).astype(jnp.float32)


def draw_log_decay(key, part):
    sluggish_mask = slow_heads(key)
    horizon = jax.random.uniform(jax.random.fold_in(key, 31), (VALUE_HEAD_COUNT,), jnp.float32, 30.0, 50.0)
    slow_total = jax.random.uniform(jax.random.fold_in(key, 33), (VALUE_HEAD_COUNT,), jnp.float32, 0.25, 0.5)
    baseline_rate = jnp.where(sluggish_mask, slow_total / PROMPT_TOKENS, math.log(10.0) / horizon)
    segment_log = jax.random.uniform(jax.random.fold_in(key, 37), (VALUE_HEAD_COUNT, PROMPT_TOKENS // TOK_DEV), jnp.float32, math.log(0.7), math.log(1.4))
    section_factor = jnp.repeat(jnp.exp(segment_log), TOK_DEV, axis=1)
    token_noise = jax.random.uniform(jax.random.fold_in(key, 39), (VALUE_HEAD_COUNT, PROMPT_TOKENS), jnp.float32, 0.5, 1.5)
    spike_positions = jax.random.randint(jax.random.fold_in(key, 41), (VALUE_HEAD_COUNT, 2), 0, PROMPT_TOKENS)
    spike_depth = jax.random.uniform(jax.random.fold_in(key, 43), (VALUE_HEAD_COUNT, 2), jnp.float32, 0.223, 0.4)
    token_positions = jnp.arange(PROMPT_TOKENS, dtype=jnp.int32)
    spike_loss = jnp.where(token_positions[None, :] == spike_positions[:, 0:1], spike_depth[:, 0:1], 0.0)
    spike_loss = spike_loss + jnp.where(token_positions[None, :] == spike_positions[:, 1:2], spike_depth[:, 1:2], 0.0)
    spike_loss = jnp.where(sluggish_mask[:, None], spike_loss, 0.0)
    return (-(baseline_rate[:, None] * section_factor * token_noise) - spike_loss).astype(jnp.float32)


def block_scale(own_key, dims, cuts, smallest, top_value):
    loudness, own = 1.0, jax.random.fold_in(own_key, 6)
    for dim, blocks in cuts:
        draws = jnp.exp(jax.random.uniform(jax.random.fold_in(own, dim), (blocks,), jnp.float32, smallest / len(cuts), top_value / len(cuts)))
        loudness = loudness * jnp.repeat(draws, dims[dim] // blocks).reshape([-1 if axis == dim else 1 for axis in range(len(dims))])
    return loudness


def bell_draw(stream_key, dims, scale, bound, cuts=(), kind=jnp.bfloat16):
    array = scale * jax.random.normal(stream_key, dims, jnp.float32)
    if cuts:
        array = array * block_scale(stream_key, dims, cuts, -0.22, 0.18)
    return jnp.clip(array, -bound, bound).astype(kind)


def setup_inputs(seed: int = 0) -> dict:
    arg_keys = jax.random.split(jax.random.key(seed), 9)
    queries = bell_draw(arg_keys[0], (PROMPT_TOKENS, HK * DK), 1.0, 6.0, ((0, 128), (1, 2)))
    key_rows = bell_draw(arg_keys[1], (PROMPT_TOKENS, HK * DK), 1.0, 6.0, ((0, 128), (1, 2)))
    values = bell_draw(arg_keys[2], (PROMPT_TOKENS, VALUE_HEAD_COUNT * DV), 1.0, 6.0, ((0, 128), (1, 2)))
    out_gate = bell_draw(arg_keys[3], (PROMPT_TOKENS, VALUE_HEAD_COUNT * DV), 1.0, 6.0, ((0, 128), (1, 2)))
    write_rate = draw_write_rate(jax.random.fold_in(arg_keys[8], 71), 0)
    log_decay = draw_log_decay(jax.random.fold_in(arg_keys[8], 71), 0)
    norm_gain = jnp.clip(1.0 + 0.18 * jax.random.normal(arg_keys[6], (DV,), jnp.float32), 0.1, 1.9)
    out_weight = bell_draw(arg_keys[7], (VALUE_HEAD_COUNT * DV, D), (VALUE_HEAD_COUNT * DV) ** -0.5, 0.125, ((0, 2),))
    return {"queries": queries, "key_rows": key_rows, "values": values, "out_gate": out_gate, "write_rate": write_rate, "log_decay": log_decay, "norm_gain": norm_gain, "out_weight": out_weight}


epsilon = 1e-06
highest = lax.Precision.HIGHEST

def unit_rows(vectors):
    return vectors / jnp.sqrt(lax.optimization_barrier(jnp.sum(vectors * vectors, axis=-1, keepdims=True)) + epsilon)

def head_blocks(row_data, head_count, head_width, repeat, normalize):
    row_count = row_data.shape[0]
    vectors = row_data.astype(jnp.float32).reshape(row_count, head_count, head_width)
    if normalize:
        vectors = unit_rows(vectors)
    vectors = jnp.repeat(vectors, repeat, axis=1)
    return vectors.reshape(row_count // SPAN, SPAN, head_count * repeat, head_width).transpose(0, 2, 1, 3)

def block_terms(query_blk, key_blk, value_blk, rate_blk, decay_blk):
    length = query_blk.shape[-2]
    log_sums = jnp.cumsum(decay_blk, axis=-1)
    row_ids = lax.broadcasted_iota(jnp.int32, (length, length), 0)
    col_ids = lax.broadcasted_iota(jnp.int32, (length, length), 1)
    lower_mask = row_ids >= col_ids
    strict_mask = row_ids > col_ids
    log_gap = log_sums[..., :, None] - log_sums[..., None, :]
    decay_mat = jnp.where(lower_mask, jnp.exp(jnp.where(lower_mask, log_gap, 0.0)), 0.0)
    key_dots = jnp.einsum('...id,...jd->...ij', key_blk, key_blk, precision=highest)
    coupling = jnp.where(strict_mask, rate_blk[..., :, None] * key_dots * decay_mat, 0.0)
    scores = jnp.einsum('...id,...jd->...ij', query_blk, key_blk, precision=highest) * decay_mat
    growth = jnp.exp(log_sums)
    right_sides = jnp.concatenate([rate_blk[..., None] * value_blk, (rate_blk * growth)[..., None] * key_blk], axis=-1)
    powered = coupling
    solved = right_sides - jnp.einsum('...ij,...jd->...id', powered, right_sides, precision=highest)
    for doubling in range(length.bit_length() - 2):
        powered = jnp.einsum('...ij,...jk->...ik', powered, powered, precision=highest)
        solved = solved + jnp.einsum('...ij,...jd->...id', powered, solved, precision=highest)
    value_width = value_blk.shape[-1]
    updates = solved[..., :value_width]
    weights = solved[..., value_width:]
    log_total = log_sums[..., -1:]
    key_decay = key_blk * jnp.exp(log_total - log_sums)[..., None]
    query_decay = query_blk * growth[..., None]
    keep_rate = jnp.exp(log_total)[..., None]
    return (updates, weights, scores, query_decay, key_decay, keep_rate)

def block_advance(memory, pieces):
    updates, weights, scores, query_decay, key_decay, keep_rate = pieces
    residue = updates - jnp.einsum('...cd,...de->...ce', weights, memory, precision=highest)
    output = jnp.einsum('...cd,...de->...ce', query_decay, memory, precision=highest) + jnp.einsum('...ij,...je->...ie', scores, residue, precision=highest)
    memory = keep_rate * memory + jnp.einsum('...cd,...ce->...de', key_decay, residue, precision=highest)
    return (memory, output)

def gated_norm(output, gate_vals, gain_row):
    inverse = lax.rsqrt(lax.optimization_barrier(jnp.mean(output * output, axis=-1, keepdims=True)) + epsilon)
    return (output * inverse * gain_row * jax.nn.silu(gate_vals)).astype(jnp.bfloat16)

def reference(queries, key_rows, values, out_gate, write_rate, log_decay, norm_gain, out_weight):
    total_rows = queries.shape[0]
    blocks = total_rows // SPAN
    repeat = VALUE_HEAD_COUNT // HK
    sliced = (queries.reshape(blocks, SPAN, HK * DK), key_rows.reshape(blocks, SPAN, HK * DK), values.reshape(blocks, SPAN, VALUE_HEAD_COUNT * DV), out_gate.reshape(blocks, SPAN, VALUE_HEAD_COUNT * DV), write_rate.reshape(VALUE_HEAD_COUNT, blocks, SPAN).transpose(1, 0, 2), log_decay.reshape(VALUE_HEAD_COUNT, blocks, SPAN).transpose(1, 0, 2))

    def advance(memory, inputs):
        query_in, key_in, value_in, gate_in, rate_in, decay_in = inputs
        query_blk = head_blocks(query_in, HK, DK, repeat, True)[0] * DK ** (-0.5)
        key_blk = head_blocks(key_in, HK, DK, repeat, True)[0]
        value_blk = head_blocks(value_in, VALUE_HEAD_COUNT, DV, 1, False)[0]
        pieces = block_terms(query_blk, key_blk, value_blk, rate_in, decay_in)
        memory, output = block_advance(memory, pieces)
        gate_vals = gate_in.astype(jnp.float32).reshape(SPAN, VALUE_HEAD_COUNT, DV)
        normed = gated_norm(output.transpose(1, 0, 2), gate_vals, norm_gain)
        return (memory, normed.reshape(SPAN, VALUE_HEAD_COUNT * DV))
    zero_memory = jnp.zeros((VALUE_HEAD_COUNT, DK, DV), jnp.float32)
    _, normed = lax.scan(advance, zero_memory, sliced)
    normed = normed.reshape(total_rows, VALUE_HEAD_COUNT * DV)
    return jnp.dot(normed, out_weight, preferred_element_type=jnp.float32).astype(jnp.bfloat16)
```

```python
import jax
import jax.numpy as jnp
from jax import lax
from jax.experimental import pallas as pl
from jax.experimental.pallas import tpu as pltpu
from jax.sharding import PartitionSpec as P

HEAD_DIM = 128
TOKENS = 128
NX, NZ, NY = 4, 8, 4
EPS = 1e-06
F32, BF16 = jnp.float32, jnp.bfloat16
MESH = pl.DeviceIdType.MESH


def mm(a, b):
    return jnp.dot(a, b, preferred_element_type=F32)


def mm_nt(a, b):
    return lax.dot_general(a, b, (((1,), (1,)), ((), ())), preferred_element_type=F32)


def compose(later, earlier):
    return earlier + later - mm(later[:, HEAD_DIM:].astype(BF16), earlier.astype(BF16))


def advance(span, state):
    return state + span[:, :HEAD_DIM] - mm(span[:, HEAD_DIM:].astype(BF16), state.astype(BF16))


def kernel(
    q_ref, k_ref, v_ref, g_ref, wr_ref, ld_ref, gain_ref, w_hbm, out_ref,
    w_vm, uw, pm, qg, pu, gated, ysend, yg, zg, pairs, xsend, xg, sm, sin, nrm, psend, precv,
    wsem, ys_sem, yr_sem, zs_sem, zr_sem, xs_sem, xr_sem, bs_sem, br_sem, ps_sem, pr_sem,
):
    me, core = lax.axis_index("seq"), lax.axis_index("head")
    y = lax.rem(me, NY)
    z = lax.rem(lax.div(me, NY), NZ)
    x = lax.div(me, NY * NZ)

    def at(x_, z_, y_):
        return {"seq": (x_ * NZ + z_) * NY + y_}

    turns = (2, 1, 3)
    owners = [lax.rem(y + d, NY) for d in turns] + [y]
    y_peers = [at(x, z, owner) for owner in owners[:3]]
    x_peers = [at(lax.rem(x + d, NX), z, y) for d in turns]
    z_up, z_down = at(x, lax.rem(z + 1, NZ), y), at(x, lax.rem(z + NZ - 1, NZ), y)
    partner = {"head": 1 - core}

    barrier = pltpu.get_barrier_semaphore()
    for peer in y_peers + x_peers + [z_up, z_down, partner]:
        pl.semaphore_signal(barrier, inc=1, device_id=peer, device_id_type=MESH)
    weights = pltpu.make_async_copy(w_hbm, w_vm, wsem)
    weights.start()

    def remote(src, dst, send, recv, peer):
        return pltpu.make_async_remote_copy(
            src_ref=src, dst_ref=dst, send_sem=send, recv_sem=recv,
            device_id=peer, device_id_type=MESH,
        )

    rows = lax.broadcasted_iota(jnp.int32, (TOKENS, TOKENS), 0)
    cols = lax.broadcasted_iota(jnp.int32, (TOKENS, TOKENS), 1)
    apart = rows ^ cols
    lower, strict, diag = rows >= cols, rows > cols, rows == cols
    eye = jnp.where(diag, 1.0, 0.0).astype(F32)

    rate = jnp.concatenate([wr_ref[pl.ds(2 * p, 2), :] for p in owners], axis=0)
    decay = jnp.concatenate([ld_ref[pl.ds(2 * p, 2), :] for p in owners], axis=0)
    log_row = jnp.dot(
        decay, jnp.where(rows <= cols, 1.0, 0.0).astype(F32),
        precision=lax.Precision.HIGHEST, preferred_element_type=F32,
    )
    columns = jnp.concatenate([log_row, rate, jnp.zeros((TOKENS - 16, TOKENS), F32)], axis=0).T

    def terms(spots):
        units = []
        for i in spots:
            off = pl.multiple_of(owners[i] * HEAD_DIM, HEAD_DIM)
            kb, qb = k_ref[:, pl.ds(off, HEAD_DIM)], q_ref[:, pl.ds(off, HEAD_DIM)]
            kf, qf = kb.astype(F32), qb.astype(F32)
            dots = mm_nt(jnp.concatenate([kb, qb], axis=0), kb)
            key_dots, query_dots = dots[:TOKENS], dots[TOKENS:]
            key_row = lax.rsqrt(jnp.sum(jnp.where(diag, key_dots, 0.0), axis=0, keepdims=True) + EPS)
            key_col = lax.rsqrt(jnp.sum(kf * kf, axis=1, keepdims=True) + EPS)
            query_col = lax.rsqrt(jnp.sum(qf * qf, axis=1, keepdims=True) + EPS) * HEAD_DIM**-0.5
            key_dots, query_dots = key_dots * key_row, query_dots * key_row
            k_t = kf.T
            for e in range(2):
                j = 2 * i + e
                log_r, log_c = log_row[j : j + 1, :], columns[:, j : j + 1]
                rate_r, rate_c = rate[j : j + 1, :], columns[:, 8 + j : 9 + j]
                fade = jnp.exp(jnp.minimum(log_c - log_r, 0.0))
                grown = jnp.exp(log_c)
                coupling = jnp.where(strict, key_dots * fade * (rate_c * key_col), 0.0)
                pm[j] = jnp.where(lower, query_dots * fade * query_col, 0.0).astype(BF16)
                qg[j] = qf * (query_col * grown)
                v_off = pl.multiple_of(owners[i] * 2 * HEAD_DIM + e * HEAD_DIM, HEAD_DIM)
                right = jnp.concatenate(
                    [v_ref[:, pl.ds(v_off, HEAD_DIM)], (kf * (key_col * grown)).astype(BF16)], axis=1
                )
                total = log_r[:, TOKENS - 1 :]
                left = (k_t * (key_row * jnp.exp(total - log_r))).astype(BF16)
                units.append([j, coupling, eye - jnp.where(apart == 1, coupling, 0.0), right, left,
                              rate_r, total])
        size = 2
        while size < TOKENS:
            band = (apart >= size) & (apart < 2 * size)
            inverses = [unit[2].astype(BF16) for unit in units]
            inner = [
                mm(jnp.where(band, unit[1], 0.0).astype(BF16), inv).astype(BF16)
                for unit, inv in zip(units, inverses)
            ]
            for unit, inv, part in zip(units, inverses, inner):
                unit[2] = unit[2] - mm(inv, part)
            size *= 2
        spans = []
        for j, _, inverse, right, left, rate_r, total in units:
            solved = mm((inverse * rate_r).astype(BF16), right).astype(BF16)
            uw[j] = solved
            span = mm(left, solved)
            keep = eye * (1.0 - jnp.exp(total))
            spans.append(
                jnp.concatenate([span[:, :HEAD_DIM], span[:, HEAD_DIM:] + keep], axis=1).astype(BF16)
            )
        return spans

    y_copies = [
        remote(ysend.at[i], yg.at[y], ys_sem.at[i], yr_sem.at[i], y_peers[i]) for i in range(3)
    ]
    first = terms((0, 1))
    for n, span in enumerate(first):
        ysend[n // 2, n % 2] = span
    pl.semaphore_wait(barrier, 9)
    y_copies[0].start()
    y_copies[1].start()
    second = terms((2, 3))
    ysend[2, 0] = second[0]
    ysend[2, 1] = second[1]
    y_copies[2].start()
    yg[y, 0] = second[2]
    yg[y, 1] = second[3]
    for copy in y_copies:
        copy.wait_recv()

    z_copies = {}

    def z_send(e, step, up):
        slot = lax.rem(z + (NZ - step if up else step), NZ)
        n = (e * 2 + (0 if up else 1)) * 4 + step
        copy = remote(zg.at[slot, e], zg.at[slot, e], zs_sem.at[n], zr_sem.at[n],
                      z_up if up else z_down)
        copy.start()
        z_copies[e, step, up] = copy

    y_spans = [[yg[j, e].astype(F32) for j in range(NY)] for e in range(2)]
    halves = [(compose(s[1], s[0]), compose(s[3], s[2])) for s in y_spans]
    for e in range(2):
        zg[z, e] = compose(halves[e][1], halves[e][0]).astype(BF16)
    for e in range(2):
        z_send(e, 0, True)
        z_send(e, 0, False)
    for e in range(2):
        sm_spans = (y_spans[e][0], halves[e][0], compose(y_spans[e][2], halves[e][0]))
        for m in range(3):
            pairs[4 + m, e] = sm_spans[m]

    def output_terms(spots):
        for i in spots:
            for e in range(2):
                j = 2 * i + e
                part = mm(pm[j], uw[j])
                pu[j] = part[:, :HEAD_DIM]
                qg[j] = qg[j] - part[:, HEAD_DIM:]
                off = pl.multiple_of(owners[i] * 2 * HEAD_DIM + e * HEAD_DIM, HEAD_DIM)
                gate = g_ref[:, pl.ds(off, HEAD_DIM)].astype(F32)
                gated[j] = gate / (1.0 + jnp.exp(-gate)) * gain_ref[...]

    for step in range(1, 4):
        if step == 1:
            output_terms((0, 1))
        elif step == 2:
            output_terms((2, 3))
        for e in range(2):
            for up in (True, False):
                z_copies[e, step - 1, up].wait_recv()
                if step < 3 or up == (e == 0):
                    z_send(e, step, up)
    for e in range(2):
        z_copies[e, 3, e == 0].wait_recv()

    x_copies = []
    quads = []
    for e in range(2):
        z_spans = [zg[j, e].astype(F32) for j in range(NZ)]
        twos = [compose(z_spans[2 * j + 1], z_spans[2 * j]) for j in range(4)]
        fours = [compose(twos[1], twos[0]), compose(twos[3], twos[2])]
        xsend[e] = compose(fours[1], fours[0]).astype(BF16)
        for d in range(3):
            n = e * 3 + d
            copy = remote(xsend.at[e], xg.at[x, e], xs_sem.at[n], xr_sem.at[n], x_peers[d])
            copy.start()
            x_copies.append(copy)
        for j in range(4):
            pairs[j, e] = twos[j]
        quads.append(fours[0])

    ahead = []
    for e in range(2):
        b2, b1, b0 = lax.div(z, 4), lax.rem(lax.div(z, 2), 2), lax.rem(z, 2)
        quad = jnp.where(b2 == 1, quads[e], 0.0)
        two = jnp.where(b1 == 1, pairs[2 * b2, e], 0.0)
        one = jnp.where(b0 == 1, zg[4 * b2 + 2 * b1, e].astype(F32), 0.0)
        ahead.append(compose(one, compose(two, quad)))

    for e in range(2):
        for d in range(3):
            x_copies[e * 3 + d].wait_recv()
        state = jnp.where(x > 0, xg[0, e, :, :HEAD_DIM].astype(F32), 0.0)
        for j in range(1, 3):
            state = jnp.where(x > j, advance(xg[j, e].astype(F32), state), state)
        state = advance(ahead[e], state)
        sm[0, e] = state.astype(BF16)
        for m in range(3):
            sm[m + 1, e] = advance(pairs[4 + m, e], state).astype(BF16)

    back = [
        remote(sm.at[owners[i]], sin.at[y], bs_sem.at[i], br_sem.at[i], y_peers[i]) for i in range(3)
    ]
    for copy in back:
        copy.start()
    sin[y] = sm[y]
    weights.wait()
    for i in (3, 2, 1, 0):
        if i < 3:
            back[(0, 1, 2)[i]].wait_recv()
        source = (owners[0], owners[2], owners[1], y)[i]
        spot = (0, 2, 1, 3)[i]
        for e in range(2):
            j = 2 * spot + e
            o = pu[j] + mm(qg[j].astype(BF16), sin[source, e])
            inv = lax.rsqrt(jnp.mean(o * o, axis=1, keepdims=True) + EPS)
            off = pl.multiple_of(source * 2 * HEAD_DIM + e * HEAD_DIM, HEAD_DIM)
            nrm[:, pl.ds(off, HEAD_DIM)] = (o * inv * gated[j]).astype(BF16)

    half = out_ref.shape[1]
    theirs = pl.multiple_of((1 - core) * half, half)
    mine = pl.multiple_of(core * half, half)
    psend[...] = mm(nrm[...], w_vm[:, pl.ds(theirs, half)]).astype(BF16)
    swap = remote(psend, precv, ps_sem, pr_sem, partner)
    swap.start()
    own = mm(nrm[...], w_vm[:, pl.ds(mine, half)])
    swap.wait_recv()
    out_ref[...] = (own + precv[...].astype(F32)).astype(BF16)
    for copy in y_copies + list(z_copies.values()) + x_copies + back + [swap]:
        copy.wait_send()


def per_device(queries, key_rows, values, out_gate, write_rate, log_decay, norm_gain, out_weight):
    tokens = queries.shape[0]
    features = out_weight.shape[1]
    vmem = pl.BlockSpec(memory_space=pltpu.VMEM)
    heads = write_rate.shape[0]
    wide = (TOKENS, 2 * HEAD_DIM)
    square = (TOKENS, HEAD_DIM)
    dma = pltpu.SemaphoreType.DMA
    return pl.pallas_call(
        kernel,
        out_shape=jax.ShapeDtypeStruct((tokens, features // 2), BF16),
        in_specs=[vmem] * 7 + [pl.BlockSpec(memory_space=pl.ANY)],
        out_specs=vmem,
        scratch_shapes=[
            pltpu.VMEM(out_weight.shape, BF16),
            pltpu.VMEM((heads,) + wide, BF16),
            pltpu.VMEM((heads,) + square, BF16),
            pltpu.VMEM((heads,) + square, F32),
            pltpu.VMEM((heads,) + square, F32),
            pltpu.VMEM((heads,) + square, F32),
            pltpu.VMEM((3, 2) + wide, BF16),
            pltpu.VMEM((NY, 2) + wide, BF16),
            pltpu.VMEM((NZ, 2) + wide, BF16),
            pltpu.VMEM((7, 2) + wide, F32),
            pltpu.VMEM((2,) + wide, BF16),
            pltpu.VMEM((NX, 2) + wide, BF16),
            pltpu.VMEM((NY, 2) + square, BF16),
            pltpu.VMEM((NY, 2) + square, BF16),
            pltpu.VMEM((tokens, heads * HEAD_DIM), BF16),
            pltpu.VMEM((tokens, features // 2), BF16),
            pltpu.VMEM((tokens, features // 2), BF16),
            dma, dma((3,)), dma((3,)), dma((16,)), dma((16,)), dma((6,)), dma((6,)),
            dma((3,)), dma((3,)), dma, dma,
        ],
        compiler_params=pltpu.CompilerParams(
            collective_id=0, has_side_effects=True, vmem_limit_bytes=48 << 20
        ),
    )(
        queries, key_rows, values, out_gate, write_rate, log_decay,
        norm_gain.reshape(1, HEAD_DIM), out_weight,
    )


def solution(mesh):
    return jax.shard_map(
        per_device,
        mesh=mesh,
        in_specs=(
            P("seq", "head"),
            P("seq", "head"),
            P("seq", "head"),
            P("seq", "head"),
            P("head", "seq"),
            P("head", "seq"),
            P(),
            P("head", None),
        ),
        out_specs=P("seq", "head"),
        check_vma=False,
    )
```

```python
import jax
import jax.numpy as jnp
from jax import lax
from jax.experimental import pallas as pl
from jax.experimental.pallas import tpu as pltpu
from jax.sharding import PartitionSpec as P

HEAD_DIM = 128
TOKENS = 128
NX, NZ, NY = 4, 8, 4
EPS = 1e-06
F32, BF16 = jnp.float32, jnp.bfloat16
MESH = pl.DeviceIdType.MESH


def mm(a, b):
    return jnp.dot(a, b, preferred_element_type=F32)


def mm_nt(a, b):
    return lax.dot_general(a, b, (((1,), (1,)), ((), ())), preferred_element_type=F32)


def compose(later, earlier):
    return earlier + later - mm(later[:, HEAD_DIM:].astype(BF16), earlier.astype(BF16))


def advance(span, state):
    return state + span[:, :HEAD_DIM] - mm(span[:, HEAD_DIM:].astype(BF16), state.astype(BF16))


def kernel(
    q_hbm, k_hbm, v_hbm, g_hbm, wr_hbm, ld_hbm, gain_hbm, w_hbm, out_ref,
    q_ref, k_ref, v_ref, g_ref, wr_ref, ld_ref, gain_ref, w_vm, uw, pm, qg, pu, gated, ysend, yg, zg, pairs, xsend, xg, sm, sin, nrm, psend, precv,
    in_sem, ys_sem, yr_sem, zs_sem, zr_sem, xs_sem, xr_sem, bs_sem, br_sem, ps_sem, pr_sem,
):
    me, core = lax.axis_index("seq"), lax.axis_index("head")
    y = lax.rem(me, NY)
    z = lax.rem(lax.div(me, NY), NZ)
    x = lax.div(me, NY * NZ)

    def at(x_, z_, y_):
        return {"seq": (x_ * NZ + z_) * NY + y_}

    turns = (2, 1, 3)
    owners = [lax.rem(y + d, NY) for d in turns] + [y]
    y_peers = [at(x, z, owner) for owner in owners[:3]]
    x_peers = [at(lax.rem(x + d, NX), z, y) for d in turns]
    z_up, z_down = at(x, lax.rem(z + 1, NZ), y), at(x, lax.rem(z + NZ - 1, NZ), y)
    partner = {"head": 1 - core}

    barrier = pltpu.get_barrier_semaphore()
    for peer in y_peers + x_peers + [z_up, z_down, partner]:
        pl.semaphore_signal(barrier, inc=1, device_id=peer, device_id_type=MESH)
    loads = [
        pltpu.make_async_copy(src, dst, in_sem.at[n])
        for n, (src, dst) in enumerate((
            (ld_hbm, ld_ref), (wr_hbm, wr_ref), (k_hbm, k_ref), (q_hbm, q_ref), (v_hbm, v_ref),
            (g_hbm, g_ref), (gain_hbm, gain_ref), (w_hbm, w_vm),
        ))
    ]
    for load in loads:
        load.start()

    def remote(src, dst, send, recv, peer):
        return pltpu.make_async_remote_copy(
            src_ref=src, dst_ref=dst, send_sem=send, recv_sem=recv,
            device_id=peer, device_id_type=MESH,
        )

    rows = lax.broadcasted_iota(jnp.int32, (TOKENS, TOKENS), 0)
    cols = lax.broadcasted_iota(jnp.int32, (TOKENS, TOKENS), 1)
    apart = rows ^ cols
    lower, strict, diag = rows >= cols, rows > cols, rows == cols
    eye = jnp.where(diag, 1.0, 0.0).astype(F32)

    for load in loads[:2]:
        load.wait()
    rate = jnp.concatenate([wr_ref[pl.ds(2 * p, 2), :] for p in owners], axis=0)
    decay = jnp.concatenate([ld_ref[pl.ds(2 * p, 2), :] for p in owners], axis=0)
    log_row = jnp.dot(
        decay, jnp.where(rows <= cols, 1.0, 0.0).astype(F32),
        precision=lax.Precision.HIGHEST, preferred_element_type=F32,
    )
    columns = jnp.concatenate([log_row, rate, jnp.zeros((TOKENS - 16, TOKENS), F32)], axis=0).T

    def terms(spots):
        units = []
        for i in spots:
            off = pl.multiple_of(owners[i] * HEAD_DIM, HEAD_DIM)
            kb, qb = k_ref[:, pl.ds(off, HEAD_DIM)], q_ref[:, pl.ds(off, HEAD_DIM)]
            kf, qf = kb.astype(F32), qb.astype(F32)
            dots = mm_nt(jnp.concatenate([kb, qb], axis=0), kb)
            key_dots, query_dots = dots[:TOKENS], dots[TOKENS:]
            key_row = lax.rsqrt(jnp.sum(jnp.where(diag, key_dots, 0.0), axis=0, keepdims=True) + EPS)
            key_col = lax.rsqrt(jnp.sum(kf * kf, axis=1, keepdims=True) + EPS)
            query_col = lax.rsqrt(jnp.sum(qf * qf, axis=1, keepdims=True) + EPS) * HEAD_DIM**-0.5
            key_dots, query_dots = key_dots * key_row, query_dots * key_row
            k_t = kf.T
            for e in range(2):
                j = 2 * i + e
                log_r, log_c = log_row[j : j + 1, :], columns[:, j : j + 1]
                rate_r, rate_c = rate[j : j + 1, :], columns[:, 8 + j : 9 + j]
                fade = jnp.exp(jnp.minimum(log_c - log_r, 0.0))
                grown = jnp.exp(log_c)
                coupling = jnp.where(strict, key_dots * fade * (rate_c * key_col), 0.0)
                pm[j] = jnp.where(lower, query_dots * fade * query_col, 0.0).astype(BF16)
                qg[j] = qf * (query_col * grown)
                v_off = pl.multiple_of(owners[i] * 2 * HEAD_DIM + e * HEAD_DIM, HEAD_DIM)
                right = jnp.concatenate(
                    [v_ref[:, pl.ds(v_off, HEAD_DIM)], (kf * (key_col * grown)).astype(BF16)], axis=1
                )
                total = log_r[:, TOKENS - 1 :]
                left = (k_t * (key_row * jnp.exp(total - log_r))).astype(BF16)
                units.append([j, coupling, eye - jnp.where(apart == 1, coupling, 0.0), right, left,
                              rate_r, total])
        size = 2
        while size < TOKENS:
            band = (apart >= size) & (apart < 2 * size)
            inverses = [unit[2].astype(BF16) for unit in units]
            inner = [
                mm(jnp.where(band, unit[1], 0.0).astype(BF16), inv).astype(BF16)
                for unit, inv in zip(units, inverses)
            ]
            for unit, inv, part in zip(units, inverses, inner):
                unit[2] = unit[2] - mm(inv, part)
            size *= 2
        spans = []
        for j, _, inverse, right, left, rate_r, total in units:
            solved = mm((inverse * rate_r).astype(BF16), right).astype(BF16)
            uw[j] = solved
            span = mm(left, solved)
            keep = eye * (1.0 - jnp.exp(total))
            spans.append(
                jnp.concatenate([span[:, :HEAD_DIM], span[:, HEAD_DIM:] + keep], axis=1).astype(BF16)
            )
        return spans

    y_copies = [
        remote(ysend.at[i], yg.at[y], ys_sem.at[i], yr_sem.at[i], y_peers[i]) for i in range(3)
    ]
    for load in loads[2:5]:
        load.wait()
    first = terms((0, 1))
    for n, span in enumerate(first):
        ysend[n // 2, n % 2] = span
    pl.semaphore_wait(barrier, 9)
    y_copies[0].start()
    y_copies[1].start()
    second = terms((2, 3))
    ysend[2, 0] = second[0]
    ysend[2, 1] = second[1]
    y_copies[2].start()
    yg[y, 0] = second[2]
    yg[y, 1] = second[3]
    for copy in y_copies:
        copy.wait_recv()

    z_copies = {}

    def z_send(e, step, up):
        slot = lax.rem(z + (NZ - step if up else step), NZ)
        n = (e * 2 + (0 if up else 1)) * 4 + step
        copy = remote(zg.at[slot, e], zg.at[slot, e], zs_sem.at[n], zr_sem.at[n],
                      z_up if up else z_down)
        copy.start()
        z_copies[e, step, up] = copy

    y_spans = [[yg[j, e].astype(F32) for j in range(NY)] for e in range(2)]
    halves = [(compose(s[1], s[0]), compose(s[3], s[2])) for s in y_spans]
    for e in range(2):
        zg[z, e] = compose(halves[e][1], halves[e][0]).astype(BF16)
    for e in range(2):
        z_send(e, 0, True)
        z_send(e, 0, False)
    for e in range(2):
        sm_spans = (y_spans[e][0], halves[e][0], compose(y_spans[e][2], halves[e][0]))
        for m in range(3):
            pairs[4 + m, e] = sm_spans[m]

    def output_terms(spots):
        for i in spots:
            for e in range(2):
                j = 2 * i + e
                part = mm(pm[j], uw[j])
                pu[j] = part[:, :HEAD_DIM]
                qg[j] = qg[j] - part[:, HEAD_DIM:]
                off = pl.multiple_of(owners[i] * 2 * HEAD_DIM + e * HEAD_DIM, HEAD_DIM)
                gate = g_ref[:, pl.ds(off, HEAD_DIM)].astype(F32)
                gated[j] = gate / (1.0 + jnp.exp(-gate)) * gain_ref[...]

    for load in loads[5:7]:
        load.wait()
    for step in range(1, 4):
        if step == 1:
            output_terms((0, 1))
        elif step == 2:
            output_terms((2, 3))
        for e in range(2):
            for up in (True, False):
                z_copies[e, step - 1, up].wait_recv()
                if step < 3 or up == (e == 0):
                    z_send(e, step, up)
    for e in range(2):
        z_copies[e, 3, e == 0].wait_recv()

    x_copies = []
    quads = []
    for e in range(2):
        z_spans = [zg[j, e].astype(F32) for j in range(NZ)]
        twos = [compose(z_spans[2 * j + 1], z_spans[2 * j]) for j in range(4)]
        fours = [compose(twos[1], twos[0]), compose(twos[3], twos[2])]
        xsend[e] = compose(fours[1], fours[0]).astype(BF16)
        for d in range(3):
            n = e * 3 + d
            copy = remote(xsend.at[e], xg.at[x, e], xs_sem.at[n], xr_sem.at[n], x_peers[d])
            copy.start()
            x_copies.append(copy)
        for j in range(4):
            pairs[j, e] = twos[j]
        quads.append(fours[0])

    ahead = []
    for e in range(2):
        b2, b1, b0 = lax.div(z, 4), lax.rem(lax.div(z, 2), 2), lax.rem(z, 2)
        quad = jnp.where(b2 == 1, quads[e], 0.0)
        two = jnp.where(b1 == 1, pairs[2 * b2, e], 0.0)
        one = jnp.where(b0 == 1, zg[4 * b2 + 2 * b1, e].astype(F32), 0.0)
        ahead.append(compose(one, compose(two, quad)))

    for e in range(2):
        for d in range(3):
            x_copies[e * 3 + d].wait_recv()
        state = jnp.where(x > 0, xg[0, e, :, :HEAD_DIM].astype(F32), 0.0)
        for j in range(1, 3):
            state = jnp.where(x > j, advance(xg[j, e].astype(F32), state), state)
        state = advance(ahead[e], state)
        sm[0, e] = state.astype(BF16)
        for m in range(3):
            sm[m + 1, e] = advance(pairs[4 + m, e], state).astype(BF16)

    back = [
        remote(sm.at[owners[i]], sin.at[y], bs_sem.at[i], br_sem.at[i], y_peers[i]) for i in range(3)
    ]
    for copy in back:
        copy.start()
    sin[y] = sm[y]
    loads[7].wait()
    for i in (3, 2, 1, 0):
        if i < 3:
            back[(0, 1, 2)[i]].wait_recv()
        source = (owners[0], owners[2], owners[1], y)[i]
        spot = (0, 2, 1, 3)[i]
        for e in range(2):
            j = 2 * spot + e
            o = pu[j] + mm(qg[j].astype(BF16), sin[source, e])
            inv = lax.rsqrt(jnp.mean(o * o, axis=1, keepdims=True) + EPS)
            off = pl.multiple_of(source * 2 * HEAD_DIM + e * HEAD_DIM, HEAD_DIM)
            nrm[:, pl.ds(off, HEAD_DIM)] = (o * inv * gated[j]).astype(BF16)

    half = out_ref.shape[1]
    theirs = pl.multiple_of((1 - core) * half, half)
    mine = pl.multiple_of(core * half, half)
    psend[...] = mm(nrm[...], w_vm[:, pl.ds(theirs, half)]).astype(BF16)
    swap = remote(psend, precv, ps_sem, pr_sem, partner)
    swap.start()
    own = mm(nrm[...], w_vm[:, pl.ds(mine, half)])
    swap.wait_recv()
    out_ref[...] = (own + precv[...].astype(F32)).astype(BF16)
    for copy in y_copies + list(z_copies.values()) + x_copies + back + [swap]:
        copy.wait_send()


def per_device(queries, key_rows, values, out_gate, write_rate, log_decay, norm_gain, out_weight):
    tokens = queries.shape[0]
    features = out_weight.shape[1]
    hbm = pl.BlockSpec(memory_space=pltpu.HBM)
    heads = write_rate.shape[0]
    wide = (TOKENS, 2 * HEAD_DIM)
    square = (TOKENS, HEAD_DIM)
    dma = pltpu.SemaphoreType.DMA
    return pl.pallas_call(
        kernel,
        out_shape=jax.ShapeDtypeStruct((tokens, features // 2), BF16),
        in_specs=[hbm] * 8,
        out_specs=pl.BlockSpec(memory_space=pltpu.VMEM),
        scratch_shapes=[
            pltpu.VMEM(queries.shape, BF16),
            pltpu.VMEM(key_rows.shape, BF16),
            pltpu.VMEM(values.shape, BF16),
            pltpu.VMEM(out_gate.shape, BF16),
            pltpu.VMEM(write_rate.shape, F32),
            pltpu.VMEM(log_decay.shape, F32),
            pltpu.VMEM((1, HEAD_DIM), F32),
            pltpu.VMEM(out_weight.shape, BF16),
            pltpu.VMEM((heads,) + wide, BF16),
            pltpu.VMEM((heads,) + square, BF16),
            pltpu.VMEM((heads,) + square, F32),
            pltpu.VMEM((heads,) + square, F32),
            pltpu.VMEM((heads,) + square, F32),
            pltpu.VMEM((3, 2) + wide, BF16),
            pltpu.VMEM((NY, 2) + wide, BF16),
            pltpu.VMEM((NZ, 2) + wide, BF16),
            pltpu.VMEM((7, 2) + wide, F32),
            pltpu.VMEM((2,) + wide, BF16),
            pltpu.VMEM((NX, 2) + wide, BF16),
            pltpu.VMEM((NY, 2) + square, BF16),
            pltpu.VMEM((NY, 2) + square, BF16),
            pltpu.VMEM((tokens, heads * HEAD_DIM), BF16),
            pltpu.VMEM((tokens, features // 2), BF16),
            pltpu.VMEM((tokens, features // 2), BF16),
            dma((8,)), dma((3,)), dma((3,)), dma((16,)), dma((16,)), dma((6,)), dma((6,)),
            dma((3,)), dma((3,)), dma, dma,
        ],
        compiler_params=pltpu.CompilerParams(
            collective_id=0, has_side_effects=True, vmem_limit_bytes=67_043_328
        ),
    )(
        queries, key_rows, values, out_gate, write_rate, log_decay,
        norm_gain.reshape(1, HEAD_DIM), out_weight,
    )


def solution(mesh):
    return jax.shard_map(
        per_device,
        mesh=mesh,
        in_specs=(
            P("seq", "head"),
            P("seq", "head"),
            P("seq", "head"),
            P("seq", "head"),
            P("head", "seq"),
            P("head", "seq"),
            P(),
            P("head", None),
        ),
        out_specs=P("seq", "head"),
        check_vma=False,
    )
```

```python
import jax
import jax.numpy as jnp
from jax import lax
from jax.experimental import pallas as pl
from jax.experimental.pallas import tpu as pltpu
from jax.sharding import PartitionSpec as P

HEAD_DIM = 128
TOKENS = 128
NX, NZ, NY = 4, 8, 4
EPS = 1e-06
F32, BF16 = jnp.float32, jnp.bfloat16
MESH = pl.DeviceIdType.MESH


def mm(a, b):
    return jnp.dot(a, b, preferred_element_type=F32)


def mm_nt(a, b):
    return lax.dot_general(a, b, (((1,), (1,)), ((), ())), preferred_element_type=F32)


def compose(later, earlier):
    return earlier + later - mm(later[:, HEAD_DIM:].astype(BF16), earlier.astype(BF16))


def advance(span, state):
    return state + span[:, :HEAD_DIM] - mm(span[:, HEAD_DIM:].astype(BF16), state.astype(BF16))


def kernel(
    q_hbm, k_hbm, v_hbm, g_hbm, wr_hbm, ld_hbm, gain_hbm, w_hbm, out_ref,
    q_ref, k_ref, v_ref, g_ref, wr_ref, ld_ref, gain_ref, w_vm, uw, pm, qg, pu, gated,
    ysend, yg, zg, before, xsend, xg, sm, sin, nrm, psend, precv,
    in_sem, ys_sem, yr_sem, zs_sem, zr_sem, xs_sem, xr_sem, bs_sem, br_sem, ps_sem, pr_sem,
):
    me, core = lax.axis_index("seq"), lax.axis_index("head")
    y = lax.rem(me, NY)
    z = lax.rem(lax.div(me, NY), NZ)
    x = lax.div(me, NY * NZ)

    def at(x_, z_, y_):
        return {"seq": (x_ * NZ + z_) * NY + y_}

    zp, ze = lax.div(z, 2), lax.rem(z, 2)
    turns = (2, 1, 3, 0)
    owners = [lax.rem(y + d, NY) for d in turns]
    sides = [ze, 1 - ze]
    others = [(i, f) for i in range(NY) for f in range(2) if (i, f) != (3, 0)]
    members = {(i, f): at(x, 2 * zp + sides[f], owners[i]) for i, f in others}
    place = 4 * ze + y
    x_peers = [at(lax.rem(x + d, NX), z, y) for d in (2, 1, 3)]
    z_peers = [at(x, 2 * lax.rem(zp + d, 4) + ze, y) for d in (2, 1, 3)]
    partner = {"head": 1 - core}

    barrier = pltpu.get_barrier_semaphore()
    signalled = list(members.values()) + x_peers + z_peers + [partner]
    for peer in signalled:
        pl.semaphore_signal(barrier, inc=1, device_id=peer, device_id_type=MESH)
    loads = [
        pltpu.make_async_copy(src, dst, in_sem.at[n])
        for n, (src, dst) in enumerate((
            (ld_hbm, ld_ref), (wr_hbm, wr_ref), (k_hbm, k_ref), (q_hbm, q_ref), (v_hbm, v_ref),
            (g_hbm, g_ref), (gain_hbm, gain_ref), (w_hbm, w_vm),
        ))
    ]
    for load in loads:
        load.start()

    def remote(src, dst, send, recv, peer):
        return pltpu.make_async_remote_copy(
            src_ref=src, dst_ref=dst, send_sem=send, recv_sem=recv,
            device_id=peer, device_id_type=MESH,
        )

    rows = lax.broadcasted_iota(jnp.int32, (TOKENS, TOKENS), 0)
    cols = lax.broadcasted_iota(jnp.int32, (TOKENS, TOKENS), 1)
    apart = rows ^ cols
    lower, strict, diag = rows >= cols, rows > cols, rows == cols
    eye = jnp.where(diag, 1.0, 0.0).astype(F32)

    for load in loads[:2]:
        load.wait()
    rate = jnp.concatenate([wr_ref[pl.ds(2 * p, 2), :] for p in owners], axis=0)
    decay = jnp.concatenate([ld_ref[pl.ds(2 * p, 2), :] for p in owners], axis=0)
    log_row = jnp.dot(
        decay, jnp.where(rows <= cols, 1.0, 0.0).astype(F32),
        precision=lax.Precision.HIGHEST, preferred_element_type=F32,
    )
    columns = jnp.concatenate([log_row, rate, jnp.zeros((TOKENS - 16, TOKENS), F32)], axis=0).T

    def terms(spots):
        units = []
        for i in spots:
            off = pl.multiple_of(owners[i] * HEAD_DIM, HEAD_DIM)
            kb, qb = k_ref[:, pl.ds(off, HEAD_DIM)], q_ref[:, pl.ds(off, HEAD_DIM)]
            kf, qf = kb.astype(F32), qb.astype(F32)
            dots = mm_nt(jnp.concatenate([kb, qb], axis=0), kb)
            key_dots, query_dots = dots[:TOKENS], dots[TOKENS:]
            key_row = lax.rsqrt(jnp.sum(jnp.where(diag, key_dots, 0.0), axis=0, keepdims=True) + EPS)
            key_col = lax.rsqrt(jnp.sum(kf * kf, axis=1, keepdims=True) + EPS)
            query_col = lax.rsqrt(jnp.sum(qf * qf, axis=1, keepdims=True) + EPS) * HEAD_DIM**-0.5
            key_dots, query_dots = key_dots * key_row, query_dots * key_row
            k_t = kf.T
            for e in range(2):
                j = 2 * i + e
                log_r, log_c = log_row[j : j + 1, :], columns[:, j : j + 1]
                rate_r, rate_c = rate[j : j + 1, :], columns[:, 8 + j : 9 + j]
                fade = jnp.exp(jnp.minimum(log_c - log_r, 0.0))
                grown = jnp.exp(log_c)
                coupling = jnp.where(strict, key_dots * fade * (rate_c * key_col), 0.0)
                pm[j] = jnp.where(lower, query_dots * fade * query_col, 0.0).astype(BF16)
                qg[j] = qf * (query_col * grown)
                v_off = pl.multiple_of(owners[i] * 2 * HEAD_DIM + e * HEAD_DIM, HEAD_DIM)
                right = jnp.concatenate(
                    [v_ref[:, pl.ds(v_off, HEAD_DIM)], (kf * (key_col * grown)).astype(BF16)], axis=1
                )
                total = log_r[:, TOKENS - 1 :]
                left = (k_t * (key_row * jnp.exp(total - log_r))).astype(BF16)
                units.append([j, coupling, eye - jnp.where(apart == 1, coupling, 0.0), right, left,
                              rate_r, total])
        size = 2
        while size < TOKENS:
            band = (apart >= size) & (apart < 2 * size)
            inverses = [unit[2].astype(BF16) for unit in units]
            inner = [
                mm(jnp.where(band, unit[1], 0.0).astype(BF16), inv).astype(BF16)
                for unit, inv in zip(units, inverses)
            ]
            for unit, inv, part in zip(units, inverses, inner):
                unit[2] = unit[2] - mm(inv, part)
            size *= 2
        spans = []
        for j, _, inverse, right, left, rate_r, total in units:
            solved = mm((inverse * rate_r).astype(BF16), right).astype(BF16)
            uw[j] = solved
            span = mm(left, solved)
            keep = eye * (1.0 - jnp.exp(total))
            spans.append(
                jnp.concatenate([span[:, :HEAD_DIM], span[:, HEAD_DIM:] + keep], axis=1).astype(BF16)
            )
        return spans

    def copies_of(source, target, send, recv):
        return {
            (i, f): remote(source(i, f), target, send.at[2 * i + f], recv.at[2 * i + f], members[i, f])
            for i, f in others
        }

    y_copies = copies_of(
        lambda i, f: ysend.at[i, sides[f]], yg.at[place], ys_sem, yr_sem
    )
    for load in loads[2:5]:
        load.wait()
    for n, span in enumerate(terms((0, 1))):
        ysend[n // 2, n % 2] = span
    pl.semaphore_wait(barrier, len(signalled))
    for key in ((0, 0), (0, 1), (1, 0), (1, 1)):
        y_copies[key].start()
    for n, span in enumerate(terms((2, 3))):
        ysend[2 + n // 2, n % 2] = span
    for key in ((2, 0), (2, 1), (3, 1)):
        y_copies[key].start()
    yg[place] = ysend[3, ze]
    for key in others:
        y_copies[key].wait_recv()

    ones = [yg[g].astype(F32) for g in range(8)]
    twos = [compose(ones[2 * g + 1], ones[2 * g]) for g in range(4)]
    fours = [compose(twos[1], twos[0]), compose(twos[3], twos[2])]
    zg[zp] = compose(fours[1], fours[0]).astype(BF16)
    z_copies = [
        remote(zg.at[zp], zg.at[zp], zs_sem.at[d], zr_sem.at[d], z_peers[d]) for d in range(3)
    ]
    for copy in z_copies:
        copy.start()
    six = compose(twos[2], fours[0])
    for g, span in enumerate((
        ones[0], twos[0], compose(ones[2], twos[0]), fours[0], compose(ones[4], fours[0]), six,
        compose(ones[6], six),
    )):
        before[g] = span

    def output_terms(spots):
        for i in spots:
            for e in range(2):
                j = 2 * i + e
                part = mm(pm[j], uw[j])
                pu[j] = part[:, :HEAD_DIM]
                qg[j] = qg[j] - part[:, HEAD_DIM:]
                off = pl.multiple_of(owners[i] * 2 * HEAD_DIM + e * HEAD_DIM, HEAD_DIM)
                gate = g_ref[:, pl.ds(off, HEAD_DIM)].astype(F32)
                gated[j] = gate / (1.0 + jnp.exp(-gate)) * gain_ref[...]

    for load in loads[5:7]:
        load.wait()
    output_terms(range(NY))
    for copy in z_copies:
        copy.wait_recv()

    z_spans = [zg[j].astype(F32) for j in range(4)]
    first_two = compose(z_spans[1], z_spans[0])
    xsend[...] = compose(compose(z_spans[3], z_spans[2]), first_two).astype(BF16)
    x_copies = [
        remote(xsend, xg.at[x], xs_sem.at[d], xr_sem.at[d], x_peers[d]) for d in range(3)
    ]
    for copy in x_copies:
        copy.start()
    b1, b0 = lax.div(zp, 2), lax.rem(zp, 2)
    ahead = compose(
        jnp.where(b0 == 1, zg[2 * b1].astype(F32), 0.0), jnp.where(b1 == 1, first_two, 0.0)
    )
    for copy in x_copies:
        copy.wait_recv()
    state = jnp.where(x > 0, xg[0, :, :HEAD_DIM].astype(F32), 0.0)
    for j in range(1, 3):
        state = jnp.where(x > j, advance(xg[j].astype(F32), state), state)
    state = advance(ahead, state)
    sm[0] = state.astype(BF16)
    for g in range(7):
        sm[g + 1] = advance(before[g], state).astype(BF16)

    back = copies_of(
        lambda i, f: sm.at[4 * sides[f] + owners[i]], sin.at[2 * y + ze], bs_sem, br_sem
    )
    for i in (0, 1, 2, 3):
        for f in range(2):
            if (i, f) in back:
                back[i, f].start()
    sin[2 * y + ze] = sm[place]
    loads[7].wait()
    for i, f in ((3, 0), (3, 1), (1, 0), (2, 0), (1, 1), (2, 1), (0, 0), (0, 1)):
        if (i, f) in back:
            back[i, f].wait_recv()
        spot = (0, 2, 1, 3)[i]
        j = 2 * spot + sides[f]
        o = pu[j] + mm(qg[j].astype(BF16), sin[2 * owners[spot] + sides[f]])
        inv = lax.rsqrt(jnp.mean(o * o, axis=1, keepdims=True) + EPS)
        off = pl.multiple_of((2 * owners[spot] + sides[f]) * HEAD_DIM, HEAD_DIM)
        nrm[:, pl.ds(off, HEAD_DIM)] = (o * inv * gated[j]).astype(BF16)

    half = out_ref.shape[1]
    theirs = pl.multiple_of((1 - core) * half, half)
    mine = pl.multiple_of(core * half, half)
    psend[...] = mm(nrm[...], w_vm[:, pl.ds(theirs, half)]).astype(BF16)
    swap = remote(psend, precv, ps_sem, pr_sem, partner)
    swap.start()
    own = mm(nrm[...], w_vm[:, pl.ds(mine, half)])
    swap.wait_recv()
    out_ref[...] = (own + precv[...].astype(F32)).astype(BF16)
    for copy in list(y_copies.values()) + z_copies + x_copies + list(back.values()) + [swap]:
        copy.wait_send()


def per_device(queries, key_rows, values, out_gate, write_rate, log_decay, norm_gain, out_weight):
    tokens = queries.shape[0]
    features = out_weight.shape[1]
    hbm = pl.BlockSpec(memory_space=pltpu.HBM)
    heads = write_rate.shape[0]
    wide = (TOKENS, 2 * HEAD_DIM)
    square = (TOKENS, HEAD_DIM)
    dma = pltpu.SemaphoreType.DMA
    return pl.pallas_call(
        kernel,
        out_shape=jax.ShapeDtypeStruct((tokens, features // 2), BF16),
        in_specs=[hbm] * 8,
        out_specs=pl.BlockSpec(memory_space=pltpu.VMEM),
        scratch_shapes=[
            pltpu.VMEM(queries.shape, BF16),
            pltpu.VMEM(key_rows.shape, BF16),
            pltpu.VMEM(values.shape, BF16),
            pltpu.VMEM(out_gate.shape, BF16),
            pltpu.VMEM(write_rate.shape, F32),
            pltpu.VMEM(log_decay.shape, F32),
            pltpu.VMEM((1, HEAD_DIM), F32),
            pltpu.VMEM(out_weight.shape, BF16),
            pltpu.VMEM((heads,) + wide, BF16),
            pltpu.VMEM((heads,) + square, BF16),
            pltpu.VMEM((heads,) + square, F32),
            pltpu.VMEM((heads,) + square, F32),
            pltpu.VMEM((heads,) + square, F32),
            pltpu.VMEM((NY, 2) + wide, BF16),
            pltpu.VMEM((8,) + wide, BF16),
            pltpu.VMEM((4,) + wide, BF16),
            pltpu.VMEM((7,) + wide, F32),
            pltpu.VMEM(wide, BF16),
            pltpu.VMEM((NX,) + wide, BF16),
            pltpu.VMEM((8,) + square, BF16),
            pltpu.VMEM((8,) + square, BF16),
            pltpu.VMEM((tokens, heads * HEAD_DIM), BF16),
            pltpu.VMEM((tokens, features // 2), BF16),
            pltpu.VMEM((tokens, features // 2), BF16),
            dma((8,)), dma((8,)), dma((8,)), dma((3,)), dma((3,)), dma((3,)), dma((3,)),
            dma((8,)), dma((8,)), dma, dma,
        ],
        compiler_params=pltpu.CompilerParams(
            collective_id=0, has_side_effects=True, vmem_limit_bytes=67_043_328
        ),
    )(
        queries, key_rows, values, out_gate, write_rate, log_decay,
        norm_gain.reshape(1, HEAD_DIM), out_weight,
    )


def solution(mesh):
    return jax.shard_map(
        per_device,
        mesh=mesh,
        in_specs=(
            P("seq", "head"),
            P("seq", "head"),
            P("seq", "head"),
            P("seq", "head"),
            P("head", "seq"),
            P("head", "seq"),
            P(),
            P("head", None),
        ),
        out_specs=P("seq", "head"),
        check_vma=False,
    )
```

```python
import jax
import jax.numpy as jnp
from jax import lax
from jax.experimental import pallas as pl
from jax.experimental.pallas import tpu as pltpu
from jax.sharding import PartitionSpec as P

HEAD_DIM = 128
TOKENS = 128
NX, NZ, NY = 4, 8, 4
EPS = 1e-06
F32, BF16 = jnp.float32, jnp.bfloat16
MESH = pl.DeviceIdType.MESH


def mm(a, b):
    return jnp.dot(a, b, preferred_element_type=F32)


def mm_nt(a, b):
    return lax.dot_general(a, b, (((1,), (1,)), ((), ())), preferred_element_type=F32)


def compose(later, earlier):
    return earlier + later - mm(later[:, HEAD_DIM:].astype(BF16), earlier.astype(BF16))


def advance(span, state):
    return state + span[:, :HEAD_DIM] - mm(span[:, HEAD_DIM:].astype(BF16), state.astype(BF16))


def kernel(
    q_hbm, k_hbm, v_hbm, g_hbm, wr_hbm, ld_hbm, gain_hbm, w_hbm, out_ref,
    q_ref, k_ref, v_ref, g_ref, wr_ref, ld_ref, gain_ref, w_vm, key_rows, uw, qe, pu, gated,
    ysend, yg, zg, before, xsend, xg, sm, sin, nrm, psend, precv,
    in_sem, ys_sem, yr_sem, zs_sem, zr_sem, xs_sem, xr_sem, bs_sem, br_sem, ps_sem, pr_sem,
):
    loads = [
        pltpu.make_async_copy(src, dst, in_sem.at[n])
        for n, (src, dst) in enumerate((
            (ld_hbm, ld_ref), (wr_hbm, wr_ref), (k_hbm, k_ref), (q_hbm, q_ref), (v_hbm, v_ref),
            (g_hbm, g_ref), (gain_hbm, gain_ref), (w_hbm, w_vm),
        ))
    ]
    for load in loads:
        load.start()

    me, core = lax.axis_index("seq"), lax.axis_index("head")
    y = lax.rem(me, NY)
    z = lax.rem(lax.div(me, NY), NZ)
    x = lax.div(me, NY * NZ)

    def at(x_, z_, y_):
        return {"seq": (x_ * NZ + z_) * NY + y_}

    zp, ze = lax.div(z, 2), lax.rem(z, 2)
    turns = (2, 1, 3, 0)
    owners = [lax.rem(y + d, NY) for d in turns]
    sides = [ze, 1 - ze]
    others = [(i, f) for i in range(NY) for f in range(2) if (i, f) != (3, 0)]
    members = {(i, f): at(x, 2 * zp + sides[f], owners[i]) for i, f in others}
    place = 4 * ze + y
    x_turns = (2, 1, 3)
    x_peers = [at(lax.rem(x + d, NX), z, y) for d in x_turns]
    z_peers = [at(x, 2 * lax.rem(zp + d, 4) + ze, y) for d in (2, 1, 3)]
    partner = {"head": 1 - core}

    barrier = pltpu.get_barrier_semaphore()
    signalled = list(members.values()) + x_peers + z_peers + [partner]
    for peer in signalled:
        pl.semaphore_signal(barrier, inc=1, device_id=peer, device_id_type=MESH)
    def remote(src, dst, send, recv, peer):
        return pltpu.make_async_remote_copy(
            src_ref=src, dst_ref=dst, send_sem=send, recv_sem=recv,
            device_id=peer, device_id_type=MESH,
        )

    rows = lax.broadcasted_iota(jnp.int32, (TOKENS, TOKENS), 0)
    cols = lax.broadcasted_iota(jnp.int32, (TOKENS, TOKENS), 1)
    apart = rows ^ cols
    lower, strict, diag = rows >= cols, rows > cols, rows == cols
    eye = jnp.where(diag, 1.0, 0.0).astype(F32)

    for load in loads[:2]:
        load.wait()
    rate = jnp.concatenate([wr_ref[pl.ds(2 * p, 2), :] for p in owners], axis=0)
    decay = jnp.concatenate([ld_ref[pl.ds(2 * p, 2), :] for p in owners], axis=0)
    log_row = jnp.dot(
        decay, jnp.where(rows <= cols, 1.0, 0.0).astype(F32),
        precision=lax.Precision.HIGHEST, preferred_element_type=F32,
    )
    columns = jnp.concatenate([log_row, rate, jnp.zeros((TOKENS - 16, TOKENS), F32)], axis=0).T

    def terms(spots):
        units = []
        for i in spots:
            off = pl.multiple_of(owners[i] * HEAD_DIM, HEAD_DIM)
            kb = k_ref[:, pl.ds(off, HEAD_DIM)]
            kf = kb.astype(F32)
            key_dots = mm_nt(kb, kb)
            key_row = lax.rsqrt(jnp.sum(jnp.where(diag, key_dots, 0.0), axis=0, keepdims=True) + EPS)
            key_col = lax.rsqrt(jnp.sum(kf * kf, axis=1, keepdims=True) + EPS)
            key_dots = key_dots * key_row
            key_rows[i : i + 1, :] = key_row
            k_t = kf.T
            for e in range(2):
                j = 2 * i + e
                log_r, log_c = log_row[j : j + 1, :], columns[:, j : j + 1]
                rate_r, rate_c = rate[j : j + 1, :], columns[:, 8 + j : 9 + j]
                fade = jnp.exp(jnp.minimum(log_c - log_r, 0.0))
                grown = jnp.exp(log_c)
                coupling = jnp.where(strict, key_dots * fade * (rate_c * key_col), 0.0)
                v_off = pl.multiple_of(owners[i] * 2 * HEAD_DIM + e * HEAD_DIM, HEAD_DIM)
                right = jnp.concatenate(
                    [v_ref[:, pl.ds(v_off, HEAD_DIM)], (kf * (key_col * grown)).astype(BF16)], axis=1
                )
                total = log_r[:, TOKENS - 1 :]
                left = (k_t * (key_row * jnp.exp(total - log_r))).astype(BF16)
                units.append([j, coupling, eye - jnp.where(apart == 1, coupling, 0.0), right, left,
                              rate_r, total])
        size = 2
        while size < TOKENS:
            band = (apart >= size) & (apart < 2 * size)
            inverses = [unit[2].astype(BF16) for unit in units]
            inner = [
                mm(jnp.where(band, unit[1], 0.0).astype(BF16), inv).astype(BF16)
                for unit, inv in zip(units, inverses)
            ]
            for unit, inv, part in zip(units, inverses, inner):
                unit[2] = unit[2] - mm(inv, part)
            size *= 2
        spans = []
        for j, _, inverse, right, left, rate_r, total in units:
            solved = mm((inverse * rate_r).astype(BF16), right).astype(BF16)
            uw[j] = solved
            span = mm(left, solved)
            keep = eye * (1.0 - jnp.exp(total))
            spans.append(
                jnp.concatenate([span[:, :HEAD_DIM], span[:, HEAD_DIM:] + keep], axis=1).astype(BF16)
            )
        return spans

    def copies_of(source, target, send, recv):
        return {
            (i, f): remote(source(i, f), target, send.at[2 * i + f], recv.at[2 * i + f], members[i, f])
            for i, f in others
        }

    y_copies = copies_of(
        lambda i, f: ysend.at[i, sides[f]], yg.at[place], ys_sem, yr_sem
    )
    for load in loads[2:5]:
        load.wait()
    for n, span in enumerate(terms((0, 1))):
        ysend[n // 2, n % 2] = span
    pl.semaphore_wait(barrier, len(signalled))
    for key in ((0, 0), (0, 1), (1, 0), (1, 1)):
        y_copies[key].start()
    for n, span in enumerate(terms((2, 3))):
        ysend[2 + n // 2, n % 2] = span
    for key in ((2, 0), (2, 1), (3, 1)):
        y_copies[key].start()
    yg[place] = ysend[3, ze]
    for key in others:
        y_copies[key].wait_recv()

    ones = [yg[g].astype(F32) for g in range(8)]
    twos = [compose(ones[2 * g + 1], ones[2 * g]) for g in range(4)]
    fours = [compose(twos[1], twos[0]), compose(twos[3], twos[2])]
    zg[zp] = compose(fours[1], fours[0]).astype(BF16)
    z_copies = [
        remote(zg.at[zp], zg.at[zp], zs_sem.at[d], zr_sem.at[d], z_peers[d]) for d in range(3)
    ]
    for copy in z_copies:
        copy.start()
    six = compose(twos[2], fours[0])
    for g, span in enumerate((
        ones[0], twos[0], compose(ones[2], twos[0]), fours[0], compose(ones[4], fours[0]), six,
        compose(ones[6], six),
    )):
        before[g] = span

    def output_terms(spots):
        for i in spots:
            off = pl.multiple_of(owners[i] * HEAD_DIM, HEAD_DIM)
            kb, qb = k_ref[:, pl.ds(off, HEAD_DIM)], q_ref[:, pl.ds(off, HEAD_DIM)]
            qf = qb.astype(F32)
            query_col = lax.rsqrt(jnp.sum(qf * qf, axis=1, keepdims=True) + EPS) * HEAD_DIM**-0.5
            query_dots = mm_nt(qb, kb) * key_rows[i : i + 1, :] * query_col
            for e in range(2):
                j = 2 * i + e
                log_r, log_c = log_row[j : j + 1, :], columns[:, j : j + 1]
                fade = jnp.exp(jnp.minimum(log_c - log_r, 0.0))
                scores = jnp.where(lower, query_dots * fade, 0.0).astype(BF16)
                part = mm(scores, uw[j])
                pu[j] = part[:, :HEAD_DIM]
                qe[j] = (qf * (query_col * jnp.exp(log_c)) - part[:, HEAD_DIM:]).astype(BF16)
                off = pl.multiple_of(owners[i] * 2 * HEAD_DIM + e * HEAD_DIM, HEAD_DIM)
                gate = g_ref[:, pl.ds(off, HEAD_DIM)].astype(F32)
                gated[j] = gate / (1.0 + jnp.exp(-gate)) * gain_ref[...]

    for load in loads[5:7]:
        load.wait()
    output_terms(range(NY))
    for copy in z_copies:
        copy.wait_recv()

    z_spans = [zg[j].astype(F32) for j in range(4)]
    first_two = compose(z_spans[1], z_spans[0])
    xsend[...] = compose(compose(z_spans[3], z_spans[2]), first_two).astype(BF16)
    x_copies = [
        remote(xsend, xg.at[x], xs_sem.at[d], xr_sem.at[d], x_peers[d]) for d in range(3)
    ]
    for turn, copy in zip(x_turns, x_copies):
        pl.when(x + turn < NX)(copy.start)
    b1, b0 = lax.div(zp, 2), lax.rem(zp, 2)
    ahead = compose(
        jnp.where(b0 == 1, zg[2 * b1].astype(F32), 0.0), jnp.where(b1 == 1, first_two, 0.0)
    )
    for turn, copy in zip(x_turns, x_copies):
        pl.when(x >= turn)(copy.wait_recv)
    state = jnp.where(x > 0, xg[0, :, :HEAD_DIM].astype(F32), 0.0)
    for j in range(1, 3):
        state = jnp.where(x > j, advance(xg[j].astype(F32), state), state)
    state = advance(ahead, state)
    sm[0] = state.astype(BF16)
    for g in range(7):
        sm[g + 1] = advance(before[g], state).astype(BF16)

    back = copies_of(
        lambda i, f: sm.at[4 * sides[f] + owners[i]], sin.at[2 * y + ze], bs_sem, br_sem
    )
    for i in (0, 1, 2, 3):
        for f in range(2):
            if (i, f) in back:
                back[i, f].start()
    sin[2 * y + ze] = sm[place]
    loads[7].wait()
    for i, f in ((3, 0), (3, 1), (1, 0), (2, 0), (1, 1), (2, 1), (0, 0), (0, 1)):
        if (i, f) in back:
            back[i, f].wait_recv()
        spot = (0, 2, 1, 3)[i]
        j = 2 * spot + sides[f]
        o = pu[j] + mm(qe[j], sin[2 * owners[spot] + sides[f]])
        inv = lax.rsqrt(jnp.mean(o * o, axis=1, keepdims=True) + EPS)
        off = pl.multiple_of((2 * owners[spot] + sides[f]) * HEAD_DIM, HEAD_DIM)
        nrm[:, pl.ds(off, HEAD_DIM)] = (o * inv * gated[j]).astype(BF16)

    half = out_ref.shape[1]
    theirs = pl.multiple_of((1 - core) * half, half)
    mine = pl.multiple_of(core * half, half)
    psend[...] = mm(nrm[...], w_vm[:, pl.ds(theirs, half)]).astype(BF16)
    swap = remote(psend, precv, ps_sem, pr_sem, partner)
    swap.start()
    own = mm(nrm[...], w_vm[:, pl.ds(mine, half)])
    swap.wait_recv()
    out_ref[...] = (own + precv[...].astype(F32)).astype(BF16)
    for turn, copy in zip(x_turns, x_copies):
        pl.when(x + turn < NX)(copy.wait_send)
    for copy in list(y_copies.values()) + z_copies + list(back.values()) + [swap]:
        copy.wait_send()


def per_device(queries, key_rows, values, out_gate, write_rate, log_decay, norm_gain, out_weight):
    tokens = queries.shape[0]
    features = out_weight.shape[1]
    hbm = pl.BlockSpec(memory_space=pltpu.HBM)
    heads = write_rate.shape[0]
    wide = (TOKENS, 2 * HEAD_DIM)
    square = (TOKENS, HEAD_DIM)
    dma = pltpu.SemaphoreType.DMA
    return pl.pallas_call(
        kernel,
        out_shape=jax.ShapeDtypeStruct((tokens, features // 2), BF16),
        in_specs=[hbm] * 8,
        out_specs=pl.BlockSpec(memory_space=pltpu.VMEM),
        scratch_shapes=[
            pltpu.VMEM(queries.shape, BF16),
            pltpu.VMEM(key_rows.shape, BF16),
            pltpu.VMEM(values.shape, BF16),
            pltpu.VMEM(out_gate.shape, BF16),
            pltpu.VMEM(write_rate.shape, F32),
            pltpu.VMEM(log_decay.shape, F32),
            pltpu.VMEM((1, HEAD_DIM), F32),
            pltpu.VMEM(out_weight.shape, BF16),
            pltpu.VMEM((8, TOKENS), F32),
            pltpu.VMEM((heads,) + wide, BF16),
            pltpu.VMEM((heads,) + square, BF16),
            pltpu.VMEM((heads,) + square, F32),
            pltpu.VMEM((heads,) + square, F32),
            pltpu.VMEM((NY, 2) + wide, BF16),
            pltpu.VMEM((8,) + wide, BF16),
            pltpu.VMEM((4,) + wide, BF16),
            pltpu.VMEM((7,) + wide, F32),
            pltpu.VMEM(wide, BF16),
            pltpu.VMEM((NX,) + wide, BF16),
            pltpu.VMEM((8,) + square, BF16),
            pltpu.VMEM((8,) + square, BF16),
            pltpu.VMEM((tokens, heads * HEAD_DIM), BF16),
            pltpu.VMEM((tokens, features // 2), BF16),
            pltpu.VMEM((tokens, features // 2), BF16),
            dma((8,)), dma((8,)), dma((8,)), dma((3,)), dma((3,)), dma((3,)), dma((3,)),
            dma((8,)), dma((8,)), dma, dma,
        ],
        compiler_params=pltpu.CompilerParams(
            collective_id=0, has_side_effects=True, vmem_limit_bytes=48 << 20
        ),
    )(*(
        pltpu.with_memory_space_constraint(operand, pltpu.HBM)
        for operand in (
            queries, key_rows, values, out_gate, write_rate, log_decay,
            norm_gain.reshape(1, HEAD_DIM), out_weight,
        )
    ))


def solution(mesh):
    return jax.shard_map(
        per_device,
        mesh=mesh,
        in_specs=(
            P("seq", "head"),
            P("seq", "head"),
            P("seq", "head"),
            P("seq", "head"),
            P("head", "seq"),
            P("head", "seq"),
            P(),
            P("head", None),
        ),
        out_specs=P("seq", "head"),
        check_vma=False,
    )
```

```python
import jax
import jax.numpy as jnp
from jax import lax
from jax.experimental import pallas as pl
from jax.experimental.pallas import tpu as pltpu
from jax.sharding import PartitionSpec as P

HEAD_DIM = 128
TOKENS = 128
NX, NZ, NY = 4, 8, 4
EPS = 1e-06
F32, BF16 = jnp.float32, jnp.bfloat16
MESH = pl.DeviceIdType.MESH


def mm(a, b):
    return jnp.dot(a, b, preferred_element_type=F32)


def mm_nt(a, b):
    return lax.dot_general(a, b, (((1,), (1,)), ((), ())), preferred_element_type=F32)


def compose(later, earlier):
    return earlier + later - mm(later[:, HEAD_DIM:].astype(BF16), earlier.astype(BF16))


def advance(span, state):
    return state + span[:, :HEAD_DIM] - mm(span[:, HEAD_DIM:].astype(BF16), state.astype(BF16))


def kernel(
    q_hbm, k_hbm, v_hbm, g_hbm, wr_hbm, ld_hbm, gain_hbm, w_hbm, out_ref,
    q_ref, k_ref, v_ref, g_ref, wr_ref, ld_ref, gain_ref, w_vm, key_rows, uw, qe, pu, gated,
    ysend, yg, zg, before, xsend, xg, sm, sin, to_them, own, psend, precv,
    in_sem, ys_sem, yr_sem, zs_sem, zr_sem, xs_sem, xr_sem, bs_sem, br_sem, ps_sem, pr_sem,
):
    loads = [
        pltpu.make_async_copy(src, dst, in_sem.at[n])
        for n, (src, dst) in enumerate((
            (ld_hbm, ld_ref), (wr_hbm, wr_ref), (k_hbm, k_ref), (q_hbm, q_ref), (v_hbm, v_ref),
            (g_hbm, g_ref), (gain_hbm, gain_ref), (w_hbm, w_vm),
        ))
    ]
    for load in loads:
        load.start()

    me, core = lax.axis_index("seq"), lax.axis_index("head")
    y = lax.rem(me, NY)
    z = lax.rem(lax.div(me, NY), NZ)
    x = lax.div(me, NY * NZ)

    def at(x_, z_, y_):
        return {"seq": (x_ * NZ + z_) * NY + y_}

    zp, ze = lax.div(z, 2), lax.rem(z, 2)
    turns = (2, 1, 3, 0)
    owners = [lax.rem(y + d, NY) for d in turns]
    sides = [ze, 1 - ze]
    others = [(i, f) for i in range(NY) for f in range(2) if (i, f) != (3, 0)]
    members = {(i, f): at(x, 2 * zp + sides[f], owners[i]) for i, f in others}
    place = 4 * ze + y
    x_turns = (2, 1, 3)
    x_peers = [at(lax.rem(x + d, NX), z, y) for d in x_turns]
    z_peers = [at(x, 2 * lax.rem(zp + d, 4) + ze, y) for d in (2, 1, 3)]
    partner = {"head": 1 - core}

    barrier = pltpu.get_barrier_semaphore()
    signalled = list(members.values()) + x_peers + z_peers + [partner]
    for peer in signalled:
        pl.semaphore_signal(barrier, inc=1, device_id=peer, device_id_type=MESH)
    def remote(src, dst, send, recv, peer):
        return pltpu.make_async_remote_copy(
            src_ref=src, dst_ref=dst, send_sem=send, recv_sem=recv,
            device_id=peer, device_id_type=MESH,
        )

    rows = lax.broadcasted_iota(jnp.int32, (TOKENS, TOKENS), 0)
    cols = lax.broadcasted_iota(jnp.int32, (TOKENS, TOKENS), 1)
    apart = rows ^ cols
    lower, strict, diag = rows >= cols, rows > cols, rows == cols
    eye = jnp.where(diag, 1.0, 0.0).astype(F32)

    for load in loads[:2]:
        load.wait()
    rate = jnp.concatenate([wr_ref[pl.ds(2 * p, 2), :] for p in owners], axis=0)
    decay = jnp.concatenate([ld_ref[pl.ds(2 * p, 2), :] for p in owners], axis=0)
    log_row = jnp.dot(
        decay, jnp.where(rows <= cols, 1.0, 0.0).astype(F32),
        precision=lax.Precision.HIGHEST, preferred_element_type=F32,
    )
    columns = jnp.concatenate([log_row, rate, jnp.zeros((TOKENS - 16, TOKENS), F32)], axis=0).T

    def terms(spots):
        units = []
        for i in spots:
            off = pl.multiple_of(owners[i] * HEAD_DIM, HEAD_DIM)
            kb = k_ref[:, pl.ds(off, HEAD_DIM)]
            kf = kb.astype(F32)
            key_dots = mm_nt(kb, kb)
            key_row = lax.rsqrt(jnp.sum(jnp.where(diag, key_dots, 0.0), axis=0, keepdims=True) + EPS)
            key_col = lax.rsqrt(jnp.sum(kf * kf, axis=1, keepdims=True) + EPS)
            key_dots = key_dots * key_row
            key_rows[i : i + 1, :] = key_row
            k_t = kf.T
            for e in range(2):
                j = 2 * i + e
                log_r, log_c = log_row[j : j + 1, :], columns[:, j : j + 1]
                rate_r, rate_c = rate[j : j + 1, :], columns[:, 8 + j : 9 + j]
                fade = jnp.exp(jnp.minimum(log_c - log_r, 0.0))
                grown = jnp.exp(log_c)
                coupling = jnp.where(strict, key_dots * fade * (rate_c * key_col), 0.0)
                v_off = pl.multiple_of(owners[i] * 2 * HEAD_DIM + e * HEAD_DIM, HEAD_DIM)
                right = jnp.concatenate(
                    [v_ref[:, pl.ds(v_off, HEAD_DIM)], (kf * (key_col * grown)).astype(BF16)], axis=1
                )
                total = log_r[:, TOKENS - 1 :]
                left = (k_t * (key_row * jnp.exp(total - log_r))).astype(BF16)
                units.append([j, coupling, eye - jnp.where(apart == 1, coupling, 0.0), right, left,
                              rate_r, total])
        for size in (2, 8, 32):
            band = (apart >= size) & (apart < 4 * size)
            inverses = [unit[2].astype(BF16) for unit in units]
            steps = [
                mm(jnp.where(band, unit[1], 0.0).astype(BF16), inv).astype(BF16)
                for unit, inv in zip(units, inverses)
            ]
            squares = [
                mm(jnp.concatenate([step, inv], axis=0), step) for step, inv in zip(steps, inverses)
            ]
            for unit, square in zip(units, squares):
                unit[2] = unit[2] - square[TOKENS:]
            more = [
                mm(unit[2].astype(BF16), square[:TOKENS].astype(BF16))
                for unit, square in zip(units, squares)
            ]
            for unit, part in zip(units, more):
                unit[2] = unit[2] + part
        spans = []
        for j, _, inverse, right, left, rate_r, total in units:
            solved = mm((inverse * rate_r).astype(BF16), right).astype(BF16)
            uw[j] = solved
            span = mm(left, solved)
            keep = eye * (1.0 - jnp.exp(total))
            spans.append(
                jnp.concatenate([span[:, :HEAD_DIM], span[:, HEAD_DIM:] + keep], axis=1).astype(BF16)
            )
        return spans

    def copies_of(source, target, send, recv):
        return {
            (i, f): remote(source(i, f), target, send.at[2 * i + f], recv.at[2 * i + f], members[i, f])
            for i, f in others
        }

    y_copies = copies_of(
        lambda i, f: ysend.at[i, sides[f]], yg.at[place], ys_sem, yr_sem
    )
    for load in loads[2:5]:
        load.wait()
    for n, span in enumerate(terms((0, 1))):
        ysend[n // 2, n % 2] = span
    pl.semaphore_wait(barrier, len(signalled))
    for key in ((0, 0), (0, 1), (1, 0), (1, 1)):
        y_copies[key].start()
    for n, span in enumerate(terms((2, 3))):
        ysend[2 + n // 2, n % 2] = span
    for key in ((2, 0), (2, 1), (3, 1)):
        y_copies[key].start()
    yg[place] = ysend[3, ze]
    for key in others:
        y_copies[key].wait_recv()

    ones = [yg[g].astype(F32) for g in range(8)]
    twos = [compose(ones[2 * g + 1], ones[2 * g]) for g in range(4)]
    fours = [compose(twos[1], twos[0]), compose(twos[3], twos[2])]
    zg[zp] = compose(fours[1], fours[0]).astype(BF16)
    z_copies = [
        remote(zg.at[zp], zg.at[zp], zs_sem.at[d], zr_sem.at[d], z_peers[d]) for d in range(3)
    ]
    for copy in z_copies:
        copy.start()
    six = compose(twos[2], fours[0])
    for g, span in enumerate((
        ones[0], twos[0], compose(ones[2], twos[0]), fours[0], compose(ones[4], fours[0]), six,
        compose(ones[6], six),
    )):
        before[g] = span

    def output_terms(spots):
        for i in spots:
            off = pl.multiple_of(owners[i] * HEAD_DIM, HEAD_DIM)
            kb, qb = k_ref[:, pl.ds(off, HEAD_DIM)], q_ref[:, pl.ds(off, HEAD_DIM)]
            qf = qb.astype(F32)
            query_col = lax.rsqrt(jnp.sum(qf * qf, axis=1, keepdims=True) + EPS) * HEAD_DIM**-0.5
            query_dots = mm_nt(qb, kb) * key_rows[i : i + 1, :] * query_col
            for e in range(2):
                j = 2 * i + e
                log_r, log_c = log_row[j : j + 1, :], columns[:, j : j + 1]
                fade = jnp.exp(jnp.minimum(log_c - log_r, 0.0))
                scores = jnp.where(lower, query_dots * fade, 0.0).astype(BF16)
                part = mm(scores, uw[j])
                pu[j] = part[:, :HEAD_DIM]
                qe[j] = (qf * (query_col * jnp.exp(log_c)) - part[:, HEAD_DIM:]).astype(BF16)
                off = pl.multiple_of(owners[i] * 2 * HEAD_DIM + e * HEAD_DIM, HEAD_DIM)
                gate = g_ref[:, pl.ds(off, HEAD_DIM)].astype(F32)
                gated[j] = gate / (1.0 + jnp.exp(-gate)) * gain_ref[...]

    for load in loads[5:7]:
        load.wait()
    output_terms(range(NY))
    for copy in z_copies:
        copy.wait_recv()

    z_spans = [zg[j].astype(F32) for j in range(4)]
    first_two = compose(z_spans[1], z_spans[0])
    xsend[...] = compose(compose(z_spans[3], z_spans[2]), first_two).astype(BF16)
    x_copies = [
        remote(xsend, xg.at[x], xs_sem.at[d], xr_sem.at[d], x_peers[d]) for d in range(3)
    ]
    for turn, copy in zip(x_turns, x_copies):
        pl.when(x + turn < NX)(copy.start)
    b1, b0 = lax.div(zp, 2), lax.rem(zp, 2)
    ahead = compose(
        jnp.where(b0 == 1, zg[2 * b1].astype(F32), 0.0), jnp.where(b1 == 1, first_two, 0.0)
    )
    for g in range(7):
        before[g] = compose(before[g], ahead)
    for turn, copy in zip(x_turns, x_copies):
        pl.when(x >= turn)(copy.wait_recv)
    state = jnp.where(x > 0, xg[0, :, :HEAD_DIM].astype(F32), 0.0)
    for j in range(1, 3):
        state = jnp.where(x > j, advance(xg[j].astype(F32), state), state)
    sm[0] = advance(ahead, state).astype(BF16)
    for g in range(7):
        sm[g + 1] = advance(before[g], state).astype(BF16)

    back = copies_of(
        lambda i, f: sm.at[4 * sides[f] + owners[i]], sin.at[2 * y + ze], bs_sem, br_sem
    )
    for i in (0, 1, 2, 3):
        for f in range(2):
            if (i, f) in back:
                back[i, f].start()
    sin[2 * y + ze] = sm[place]
    loads[7].wait()
    def normed(i, f):
        if (i, f) in back:
            back[i, f].wait_recv()
        spot = (0, 2, 1, 3)[i]
        j = 2 * spot + sides[f]
        o = pu[j] + mm(qe[j], sin[2 * owners[spot] + sides[f]])
        inv = lax.rsqrt(jnp.mean(o * o, axis=1, keepdims=True) + EPS)
        out = (o * inv * gated[j]).astype(BF16)
        row = pl.multiple_of((2 * owners[spot] + sides[f]) * HEAD_DIM, HEAD_DIM)
        return out, row

    half = out_ref.shape[1]
    theirs = pl.multiple_of((1 - core) * half, half)
    mine = pl.multiple_of(core * half, half)

    def project(parts, first, count):
        left = jnp.concatenate([out for out, _ in parts], axis=1)
        return mm(left, jnp.concatenate(
            [w_vm[pl.ds(row, HEAD_DIM), pl.ds(first, count)] for _, row in parts], axis=0))

    parts = [normed(i, f) for i, f in ((3, 0), (3, 1), (1, 0), (2, 0), (1, 1), (2, 1))]
    to_them[...] = project(parts, theirs, half)
    own[...] = project(parts, mine, half)
    parts = [normed(0, 0), normed(0, 1)]
    swaps = []
    for n in range(2):
        psend[n] = (
            to_them[:, n * (half // 2) : (n + 1) * (half // 2)]
            + project(parts, pl.multiple_of(theirs + n * (half // 2), half // 2), half // 2)
        ).astype(BF16)
        swap = remote(psend.at[n], precv.at[n], ps_sem.at[n], pr_sem.at[n], partner)
        swap.start()
        swaps.append(swap)
    own[...] = own[...] + project(parts, mine, half)
    for n, swap in enumerate(swaps):
        swap.wait_recv()
        piece = pl.ds(n * (half // 2), half // 2)
        out_ref[:, piece] = (own[:, piece] + precv[n].astype(F32)).astype(BF16)
    for turn, copy in zip(x_turns, x_copies):
        pl.when(x + turn < NX)(copy.wait_send)
    for copy in list(y_copies.values()) + z_copies + list(back.values()) + swaps:
        copy.wait_send()


def per_device(queries, key_rows, values, out_gate, write_rate, log_decay, norm_gain, out_weight):
    tokens = queries.shape[0]
    features = out_weight.shape[1]
    hbm = pl.BlockSpec(memory_space=pltpu.HBM)
    heads = write_rate.shape[0]
    wide = (TOKENS, 2 * HEAD_DIM)
    square = (TOKENS, HEAD_DIM)
    dma = pltpu.SemaphoreType.DMA
    return pl.pallas_call(
        kernel,
        out_shape=jax.ShapeDtypeStruct((tokens, features // 2), BF16),
        in_specs=[hbm] * 8,
        out_specs=pl.BlockSpec(memory_space=pltpu.VMEM),
        scratch_shapes=[
            pltpu.VMEM(queries.shape, BF16),
            pltpu.VMEM(key_rows.shape, BF16),
            pltpu.VMEM(values.shape, BF16),
            pltpu.VMEM(out_gate.shape, BF16),
            pltpu.VMEM(write_rate.shape, F32),
            pltpu.VMEM(log_decay.shape, F32),
            pltpu.VMEM((1, HEAD_DIM), F32),
            pltpu.VMEM(out_weight.shape, BF16),
            pltpu.VMEM((8, TOKENS), F32),
            pltpu.VMEM((heads,) + wide, BF16),
            pltpu.VMEM((heads,) + square, BF16),
            pltpu.VMEM((heads,) + square, F32),
            pltpu.VMEM((heads,) + square, F32),
            pltpu.VMEM((NY, 2) + wide, BF16),
            pltpu.VMEM((8,) + wide, BF16),
            pltpu.VMEM((4,) + wide, BF16),
            pltpu.VMEM((7,) + wide, F32),
            pltpu.VMEM(wide, BF16),
            pltpu.VMEM((NX,) + wide, BF16),
            pltpu.VMEM((8,) + square, BF16),
            pltpu.VMEM((8,) + square, BF16),
            pltpu.VMEM((tokens, features // 2), F32),
            pltpu.VMEM((tokens, features // 2), F32),
            pltpu.VMEM((2, tokens, features // 4), BF16),
            pltpu.VMEM((2, tokens, features // 4), BF16),
            dma((8,)), dma((8,)), dma((8,)), dma((3,)), dma((3,)), dma((3,)), dma((3,)),
            dma((8,)), dma((8,)), dma((2,)), dma((2,)),
        ],
        compiler_params=pltpu.CompilerParams(
            collective_id=0, has_side_effects=True, vmem_limit_bytes=48 << 20
        ),
    )(*(
        pltpu.with_memory_space_constraint(operand, pltpu.HBM)
        for operand in (
            queries, key_rows, values, out_gate, write_rate, log_decay,
            norm_gain.reshape(1, HEAD_DIM), out_weight,
        )
    ))


def solution(mesh):
    return jax.shard_map(
        per_device,
        mesh=mesh,
        in_specs=(
            P("seq", "head"),
            P("seq", "head"),
            P("seq", "head"),
            P("seq", "head"),
            P("head", "seq"),
            P("head", "seq"),
            P(),
            P("head", None),
        ),
        out_specs=P("seq", "head"),
        check_vma=False,
    )
```

```python
import jax
import jax.numpy as jnp
from jax import lax
from jax.experimental import pallas as pl
from jax.experimental.pallas import tpu as pltpu
from jax.sharding import PartitionSpec as P

HEAD_DIM = 128
TOKENS = 128
NX, NZ, NY = 4, 8, 4
EPS = 1e-06
F32, BF16 = jnp.float32, jnp.bfloat16
MESH = pl.DeviceIdType.MESH


def mm(a, b):
    return jnp.dot(a, b, preferred_element_type=F32)


def mm_nt(a, b):
    return lax.dot_general(a, b, (((1,), (1,)), ((), ())), preferred_element_type=F32)


def compose(later, earlier):
    return earlier + later - mm(later[:, HEAD_DIM:].astype(BF16), earlier.astype(BF16))


def advance(span, state):
    return state + span[:, :HEAD_DIM] - mm(span[:, HEAD_DIM:].astype(BF16), state.astype(BF16))


def kernel(
    q_hbm, k_hbm, v_hbm, g_hbm, wr_hbm, ld_hbm, gain_hbm, w_hbm, out_ref,
    q_ref, k_ref, v_ref, g_ref, wr_ref, ld_ref, gain_ref, w_vm, key_rows, uw, qe, pu, gated,
    ysend, yg, zg, before, xsend, xg, sm, sin, to_them, own, psend, precv,
    in_sem, ys_sem, yr_sem, zs_sem, zr_sem, xs_sem, xr_sem, bs_sem, br_sem, ps_sem, pr_sem,
):
    loads = [
        pltpu.make_async_copy(src, dst, in_sem.at[n])
        for n, (src, dst) in enumerate((
            (ld_hbm, ld_ref), (wr_hbm, wr_ref), (k_hbm, k_ref), (q_hbm, q_ref), (v_hbm, v_ref),
            (g_hbm, g_ref), (gain_hbm, gain_ref), (w_hbm, w_vm),
        ))
    ]
    for load in loads:
        load.start()

    me, core = lax.axis_index("seq"), lax.axis_index("head")
    y = lax.rem(me, NY)
    z = lax.rem(lax.div(me, NY), NZ)
    x = lax.div(me, NY * NZ)

    def at(x_, z_, y_):
        return {"seq": (x_ * NZ + z_) * NY + y_}

    zp, ze = lax.div(z, 2), lax.rem(z, 2)
    turns = (2, 1, 3, 0)
    owners = [lax.rem(y + d, NY) for d in turns]
    sides = [ze, 1 - ze]
    others = [(i, f) for i in range(NY) for f in range(2) if (i, f) != (3, 0)]
    members = {(i, f): at(x, 2 * zp + sides[f], owners[i]) for i, f in others}
    place = 4 * ze + y
    x_turns = (2, 1, 3)
    x_peers = [at(lax.rem(x + d, NX), z, y) for d in x_turns]
    z_peers = [at(x, 2 * lax.rem(zp + d, 4) + ze, y) for d in (2, 1, 3)]
    partner = {"head": 1 - core}

    barrier = pltpu.get_barrier_semaphore()
    signalled = list(members.values()) + x_peers + z_peers + [partner]
    for peer in signalled:
        pl.semaphore_signal(barrier, inc=1, device_id=peer, device_id_type=MESH)
    def remote(src, dst, send, recv, peer):
        return pltpu.make_async_remote_copy(
            src_ref=src, dst_ref=dst, send_sem=send, recv_sem=recv,
            device_id=peer, device_id_type=MESH,
        )

    rows = lax.broadcasted_iota(jnp.int32, (TOKENS, TOKENS), 0)
    cols = lax.broadcasted_iota(jnp.int32, (TOKENS, TOKENS), 1)
    apart = rows ^ cols
    lower, strict, diag = rows >= cols, rows > cols, rows == cols
    eye = jnp.where(diag, 1.0, 0.0).astype(F32)

    for load in loads[:2]:
        load.wait()
    rate = jnp.concatenate([wr_ref[pl.ds(2 * p, 2), :] for p in owners], axis=0)
    decay = jnp.concatenate([ld_ref[pl.ds(2 * p, 2), :] for p in owners], axis=0)
    log_row = jnp.dot(
        decay, jnp.where(rows <= cols, 1.0, 0.0).astype(F32),
        precision=lax.Precision.HIGHEST, preferred_element_type=F32,
    )
    columns = jnp.concatenate([log_row, rate, jnp.zeros((TOKENS - 16, TOKENS), F32)], axis=0).T

    def terms(spots):
        units = []
        for i in spots:
            off = pl.multiple_of(owners[i] * HEAD_DIM, HEAD_DIM)
            kb = k_ref[:, pl.ds(off, HEAD_DIM)]
            kf = kb.astype(F32)
            key_dots = mm_nt(kb, kb)
            key_row = lax.rsqrt(jnp.sum(jnp.where(diag, key_dots, 0.0), axis=0, keepdims=True) + EPS)
            key_col = lax.rsqrt(jnp.sum(kf * kf, axis=1, keepdims=True) + EPS)
            key_dots = key_dots * key_row
            key_rows[i : i + 1, :] = key_row
            k_t = kf.T
            for e in range(2):
                j = 2 * i + e
                log_r, log_c = log_row[j : j + 1, :], columns[:, j : j + 1]
                rate_r, rate_c = rate[j : j + 1, :], columns[:, 8 + j : 9 + j]
                fade = jnp.exp(jnp.minimum(log_c - log_r, 0.0))
                grown = jnp.exp(log_c)
                coupling = jnp.where(strict, key_dots * fade * (rate_c * key_col), 0.0)
                v_off = pl.multiple_of(owners[i] * 2 * HEAD_DIM + e * HEAD_DIM, HEAD_DIM)
                right = jnp.concatenate(
                    [v_ref[:, pl.ds(v_off, HEAD_DIM)], (kf * (key_col * grown)).astype(BF16)], axis=1
                )
                total = log_r[:, TOKENS - 1 :]
                left = (k_t * (key_row * jnp.exp(total - log_r))).astype(BF16)
                units.append([j, coupling, eye - jnp.where(apart == 1, coupling, 0.0), right, left,
                              rate_r, total])
        for size in (2, 8, 32):
            band = (apart >= size) & (apart < 4 * size)
            inverses = [unit[2].astype(BF16) for unit in units]
            steps = [
                mm(jnp.where(band, unit[1], 0.0).astype(BF16), inv).astype(BF16)
                for unit, inv in zip(units, inverses)
            ]
            squares = [
                mm(jnp.concatenate([step, inv], axis=0), step) for step, inv in zip(steps, inverses)
            ]
            for unit, square in zip(units, squares):
                unit[2] = unit[2] - square[TOKENS:]
            more = [
                mm(unit[2].astype(BF16), square[:TOKENS].astype(BF16))
                for unit, square in zip(units, squares)
            ]
            for unit, part in zip(units, more):
                unit[2] = unit[2] + part
        spans = []
        for j, _, inverse, right, left, rate_r, total in units:
            solved = mm((inverse * rate_r).astype(BF16), right).astype(BF16)
            uw[j] = solved
            span = mm(left, solved)
            keep = eye * (1.0 - jnp.exp(total))
            spans.append(
                jnp.concatenate([span[:, :HEAD_DIM], span[:, HEAD_DIM:] + keep], axis=1).astype(BF16)
            )
        return spans

    def copies_of(source, target, send, recv):
        return {
            (i, f): remote(source(i, f), target, send.at[2 * i + f], recv.at[2 * i + f], members[i, f])
            for i, f in others
        }

    y_copies = copies_of(
        lambda i, f: ysend.at[i, sides[f]], yg.at[place], ys_sem, yr_sem
    )
    for load in loads[2:5]:
        load.wait()
    for n, span in enumerate(terms((0, 1))):
        ysend[n // 2, n % 2] = span
    pl.semaphore_wait(barrier, len(signalled))
    for key in ((0, 0), (0, 1), (1, 0), (1, 1)):
        y_copies[key].start()
    for n, span in enumerate(terms((2, 3))):
        ysend[2 + n // 2, n % 2] = span
    for key in ((2, 0), (2, 1), (3, 1)):
        y_copies[key].start()
    yg[place] = ysend[3, ze]
    for key in others:
        y_copies[key].wait_recv()

    ones = [yg[g].astype(F32) for g in range(8)]
    twos = [compose(ones[2 * g + 1], ones[2 * g]) for g in range(4)]
    fours = [compose(twos[1], twos[0]), compose(twos[3], twos[2])]
    zg[zp] = compose(fours[1], fours[0]).astype(BF16)
    z_copies = [
        remote(zg.at[zp], zg.at[zp], zs_sem.at[d], zr_sem.at[d], z_peers[d]) for d in range(3)
    ]
    for copy in z_copies:
        copy.start()
    six = compose(twos[2], fours[0])
    for g, span in enumerate((
        ones[0], twos[0], compose(ones[2], twos[0]), fours[0], compose(ones[4], fours[0]), six,
        compose(ones[6], six),
    )):
        before[g] = span

    def output_terms(spots):
        for i in spots:
            off = pl.multiple_of(owners[i] * HEAD_DIM, HEAD_DIM)
            kb, qb = k_ref[:, pl.ds(off, HEAD_DIM)], q_ref[:, pl.ds(off, HEAD_DIM)]
            qf = qb.astype(F32)
            query_col = lax.rsqrt(jnp.sum(qf * qf, axis=1, keepdims=True) + EPS) * HEAD_DIM**-0.5
            query_dots = mm_nt(qb, kb) * key_rows[i : i + 1, :] * query_col
            for e in range(2):
                j = 2 * i + e
                log_r, log_c = log_row[j : j + 1, :], columns[:, j : j + 1]
                fade = jnp.exp(jnp.minimum(log_c - log_r, 0.0))
                scores = jnp.where(lower, query_dots * fade, 0.0).astype(BF16)
                part = mm(scores, uw[j])
                pu[j] = part[:, :HEAD_DIM]
                qe[j] = (qf * (query_col * jnp.exp(log_c)) - part[:, HEAD_DIM:]).astype(BF16)
                off = pl.multiple_of(owners[i] * 2 * HEAD_DIM + e * HEAD_DIM, HEAD_DIM)
                gate = g_ref[:, pl.ds(off, HEAD_DIM)].astype(F32)
                gated[j] = gate / (1.0 + jnp.exp(-gate)) * gain_ref[...]

    for load in loads[5:7]:
        load.wait()
    output_terms(range(NY))
    for copy in z_copies:
        copy.wait_recv()

    z_spans = [zg[j].astype(F32) for j in range(4)]
    first_two = compose(z_spans[1], z_spans[0])
    xsend[...] = compose(compose(z_spans[3], z_spans[2]), first_two).astype(BF16)
    x_copies = [
        remote(xsend, xg.at[x], xs_sem.at[d], xr_sem.at[d], x_peers[d]) for d in range(3)
    ]
    feed = pl.ds(0, HEAD_DIM)
    x_feeds = [
        remote(xsend.at[:, feed], xg.at[x, :, feed], xs_sem.at[d], xr_sem.at[d], x_peers[d])
        for d in range(3)
    ]
    for turn, copy, short in zip(x_turns, x_copies, x_feeds):
        pl.when((x > 0) & (x + turn < NX))(copy.start)
        pl.when(x == 0)(short.start)
    b1, b0 = lax.div(zp, 2), lax.rem(zp, 2)
    ahead = compose(
        jnp.where(b0 == 1, zg[2 * b1].astype(F32), 0.0), jnp.where(b1 == 1, first_two, 0.0)
    )
    for g in range(7):
        before[g] = compose(before[g], ahead)
    for turn, copy, short in zip(x_turns, x_copies, x_feeds):
        pl.when(x > turn)(copy.wait_recv)
        pl.when(x == turn)(short.wait_recv)
    state = jnp.where(x > 0, xg[0, :, :HEAD_DIM].astype(F32), 0.0)
    for j in range(1, 3):
        state = jnp.where(x > j, advance(xg[j].astype(F32), state), state)
    sm[0] = advance(ahead, state).astype(BF16)
    for g in range(7):
        sm[g + 1] = advance(before[g], state).astype(BF16)

    back = copies_of(
        lambda i, f: sm.at[4 * sides[f] + owners[i]], sin.at[2 * y + ze], bs_sem, br_sem
    )
    for i in (0, 1, 2, 3):
        for f in range(2):
            if (i, f) in back:
                back[i, f].start()
    sin[2 * y + ze] = sm[place]
    loads[7].wait()
    def normed(i, f):
        if (i, f) in back:
            back[i, f].wait_recv()
        spot = (0, 2, 1, 3)[i]
        j = 2 * spot + sides[f]
        o = pu[j] + mm(qe[j], sin[2 * owners[spot] + sides[f]])
        inv = lax.rsqrt(jnp.mean(o * o, axis=1, keepdims=True) + EPS)
        out = (o * inv * gated[j]).astype(BF16)
        row = pl.multiple_of((2 * owners[spot] + sides[f]) * HEAD_DIM, HEAD_DIM)
        return out, row

    half = out_ref.shape[1]
    theirs = pl.multiple_of((1 - core) * half, half)
    mine = pl.multiple_of(core * half, half)

    def project(parts, first, count):
        left = jnp.concatenate([out for out, _ in parts], axis=1)
        return mm(left, jnp.concatenate(
            [w_vm[pl.ds(row, HEAD_DIM), pl.ds(first, count)] for _, row in parts], axis=0))

    parts = [normed(i, f) for i, f in ((3, 0), (3, 1), (1, 0), (2, 0), (1, 1), (2, 1))]
    to_them[...] = project(parts, theirs, half)
    own[...] = project(parts, mine, half)
    parts = [normed(0, 0), normed(0, 1)]
    swaps = []
    for n in range(2):
        psend[n] = (
            to_them[:, n * (half // 2) : (n + 1) * (half // 2)]
            + project(parts, pl.multiple_of(theirs + n * (half // 2), half // 2), half // 2)
        ).astype(BF16)
        swap = remote(psend.at[n], precv.at[n], ps_sem.at[n], pr_sem.at[n], partner)
        swap.start()
        swaps.append(swap)
    own[...] = own[...] + project(parts, mine, half)
    for n, swap in enumerate(swaps):
        swap.wait_recv()
        piece = pl.ds(n * (half // 2), half // 2)
        out_ref[:, piece] = (own[:, piece] + precv[n].astype(F32)).astype(BF16)
    for turn, copy, short in zip(x_turns, x_copies, x_feeds):
        pl.when((x > 0) & (x + turn < NX))(copy.wait_send)
        pl.when(x == 0)(short.wait_send)
    for copy in list(y_copies.values()) + z_copies + list(back.values()) + swaps:
        copy.wait_send()


def per_device(queries, key_rows, values, out_gate, write_rate, log_decay, norm_gain, out_weight):
    tokens = queries.shape[0]
    features = out_weight.shape[1]
    hbm = pl.BlockSpec(memory_space=pltpu.HBM)
    heads = write_rate.shape[0]
    wide = (TOKENS, 2 * HEAD_DIM)
    square = (TOKENS, HEAD_DIM)
    dma = pltpu.SemaphoreType.DMA
    return pl.pallas_call(
        kernel,
        out_shape=jax.ShapeDtypeStruct((tokens, features // 2), BF16),
        in_specs=[hbm] * 8,
        out_specs=pl.BlockSpec(memory_space=pltpu.VMEM),
        scratch_shapes=[
            pltpu.VMEM(queries.shape, BF16),
            pltpu.VMEM(key_rows.shape, BF16),
            pltpu.VMEM(values.shape, BF16),
            pltpu.VMEM(out_gate.shape, BF16),
            pltpu.VMEM(write_rate.shape, F32),
            pltpu.VMEM(log_decay.shape, F32),
            pltpu.VMEM((1, HEAD_DIM), F32),
            pltpu.VMEM(out_weight.shape, BF16),
            pltpu.VMEM((8, TOKENS), F32),
            pltpu.VMEM((heads,) + wide, BF16),
            pltpu.VMEM((heads,) + square, BF16),
            pltpu.VMEM((heads,) + square, F32),
            pltpu.VMEM((heads,) + square, F32),
            pltpu.VMEM((NY, 2) + wide, BF16),
            pltpu.VMEM((8,) + wide, BF16),
            pltpu.VMEM((4,) + wide, BF16),
            pltpu.VMEM((7,) + wide, F32),
            pltpu.VMEM(wide, BF16),
            pltpu.VMEM((NX,) + wide, BF16),
            pltpu.VMEM((8,) + square, BF16),
            pltpu.VMEM((8,) + square, BF16),
            pltpu.VMEM((tokens, features // 2), F32),
            pltpu.VMEM((tokens, features // 2), F32),
            pltpu.VMEM((2, tokens, features // 4), BF16),
            pltpu.VMEM((2, tokens, features // 4), BF16),
            dma((8,)), dma((8,)), dma((8,)), dma((3,)), dma((3,)), dma((3,)), dma((3,)),
            dma((8,)), dma((8,)), dma((2,)), dma((2,)),
        ],
        compiler_params=pltpu.CompilerParams(
            collective_id=0, has_side_effects=True, vmem_limit_bytes=48 << 20
        ),
    )(*(
        pltpu.with_memory_space_constraint(operand, pltpu.HBM)
        for operand in (
            queries, key_rows, values, out_gate, write_rate, log_decay,
            norm_gain.reshape(1, HEAD_DIM), out_weight,
        )
    ))


def solution(mesh):
    return jax.shard_map(
        per_device,
        mesh=mesh,
        in_specs=(
            P("seq", "head"),
            P("seq", "head"),
            P("seq", "head"),
            P("seq", "head"),
            P("head", "seq"),
            P("head", "seq"),
            P(),
            P("head", None),
        ),
        out_specs=P("seq", "head"),
        check_vma=False,
    )
```
